256 devices in a mesh: gx: 4 (over x), gy: 2 (over y_lo), ga: 32 (over y_hi, z, core).
Axes of the slice: x: 4, y: 4 (y_hi: 2, y_lo: 2; y = y_hi * 2 + y_lo), z: 8, core: 2. Of those that a mesh axis runs over, the one named last changes fastest.
Arguments:
- noise: float32 [128, 16, 256, 256], P('ga', None, 'gx', 'gy'), may hold values from 0 to 0.15
- labels: int32 [16, 256, 256], P(None, 'gx', 'gy'), may hold values from 0 to 127
- pair_class: int32 [128, 128], replicated, may hold values from 0 to 3
- class_gain: float32 [4], replicated, may hold values from 0.5 to 2
- stiffness: float32 [3, 128], P(None, 'ga'), may hold values from 0.5 to 1
- cross: float32 [128], P('ga'), may hold values from -0.4 to 0.4
- current: float32 [3, 16, 256, 256], P(None, None, 'gx', 'gy'), may hold values from -3 to 3
Outputs:
- order_out: float32 [128, 16, 256, 256], P('ga', None, 'gx', 'gy')
The draws below stay inside these ranges and needn't reach their ends.
All inputs are finite; a program needn't handle non-finite values.
Results may differ from the reference program's by a relative error of at most 0.0011.
Values may be sent and summed in bfloat16 or wider, within the bound.
A program may use at most 128 MiB of HBM per device.

```python
import jax
import jax.numpy as jnp

CLASSES = 4
NZ = 16
GRAINS = 128
NX = 256
NY = 256


def touch_ends(drawn, own_key, low, high):
    longest = drawn.shape.index(max(drawn.shape))
    spots = []
    for shift in (0, 1):
        where = [jax.random.randint(jax.random.fold_in(own_key, axis), (), 0, length) for axis, length in enumerate(drawn.shape)]
        where[longest] = (where[longest] + shift) % drawn.shape[longest]
        spots.append(tuple(where))
    return drawn.at[spots[0]].set(low).at[spots[1]].set(high)


def levels(rng, extent, split, smallest, top_value):
    def one(dim, blocks):
        draws = jax.random.uniform(jax.random.fold_in(jax.random.fold_in(rng, 6), dim), (blocks,), jnp.float32, smallest / len(split), top_value / len(split))
        return jnp.repeat(jnp.exp(draws), extent[dim] // blocks).reshape((-1,) + (1,) * (len(extent) - dim - 1))

    level = one(*split[0])
    for cut in split[1:]:
        level = level * one(*cut)
    return level


def centred(rng, shape, width, reach, pieces=(), kind=jnp.bfloat16):
    level = levels(rng, shape, pieces, -0.22, 0.18) if pieces else 1.0
    drawn = jax.random.normal(rng, shape, jnp.float32) * width * level
    return jnp.minimum(jnp.maximum(drawn, -reach), reach).astype(kind)


def setup_inputs(seed: int = 0) -> dict:
    seeds = jax.random.split(jax.random.key(seed), 8)
    noise = jnp.clip(0.15 * jax.random.uniform(seeds[0], (GRAINS, NZ, NX, NY), jnp.float32) ** levels(seeds[0], (GRAINS, NZ, NX, NY), ((0, 32), (2, 4), (3, 2)), -0.2, 0.2), 0.0, 0.15)
    labels = touch_ends(jax.random.randint(seeds[1], (NZ, NX, NY), 0, GRAINS), jax.random.fold_in(seeds[1], 1), 0, GRAINS - 1).astype(jnp.int32)
    pair_class = touch_ends(jax.random.randint(seeds[2], (GRAINS, GRAINS), 0, CLASSES), jax.random.fold_in(seeds[2], 1), 0, CLASSES - 1).astype(jnp.int32)
    class_gain = jnp.clip(jax.random.uniform(seeds[3], (CLASSES,), jnp.float32, 0.5, 2.0), 0.5, 2.0)
    stiffness = jnp.clip(0.5 + 0.5 * jax.random.uniform(seeds[4], (3, GRAINS), jnp.float32) ** levels(seeds[4], (3, GRAINS), ((1, 32),), -0.2, 0.2), 0.5, 1.0)
    cross = jnp.clip(jax.random.uniform(seeds[5], (GRAINS,), jnp.float32, -0.4, 0.4) * levels(seeds[5], (GRAINS,), ((0, 32),), -0.4, 0.0), -0.4, 0.4)
    current = centred(seeds[6], (3, NZ, NX, NY), 0.5, 3.0, ((2, 4), (3, 2)), jnp.float32)
    return {"noise": noise, "labels": labels, "pair_class": pair_class, "class_gain": class_gain, "stiffness": stiffness, "cross": cross, "current": current}


step_size = 0.1
seed_level = 0.7


def pair_matrix(pair_class, class_gain):
    classes = jnp.arange(class_gain.shape[0], dtype=jnp.int32)
    picked = jnp.sum(jnp.where(pair_class[:, :, None] == classes, class_gain, jnp.float32(0.0)), axis=2)
    symmetric = 0.5 * (picked + picked.T)
    off_diagonal = 1.0 - jnp.eye(pair_class.shape[0], dtype=jnp.float32)
    return (symmetric * off_diagonal).astype(jnp.bfloat16)


def advance(order_field, padded, coupling, stiffness, cross, current):
    center = padded[:, 1:-1, 1:-1, 1:-1]
    plus_x = padded[:, 1:-1, 2:, 1:-1]
    minus_x = padded[:, 1:-1, :-2, 1:-1]
    plus_y = padded[:, 1:-1, 1:-1, 2:]
    minus_y = padded[:, 1:-1, 1:-1, :-2]
    plus_z = padded[:, 2:, 1:-1, 1:-1]
    minus_z = padded[:, :-2, 1:-1, 1:-1]
    slope_x = 0.5 * (plus_x - minus_x)
    slope_y = 0.5 * (plus_y - minus_y)
    slope_z = 0.5 * (plus_z - minus_z)
    second_x = plus_x + minus_x - 2.0 * center
    second_y = plus_y + minus_y - 2.0 * center
    second_z = plus_z + minus_z - 2.0 * center
    mixed = 0.25 * (padded[:, 1:-1, 2:, 2:] - padded[:, 1:-1, 2:, :-2]
                    - padded[:, 1:-1, :-2, 2:] + padded[:, 1:-1, :-2, :-2])
    coef_x = stiffness[0][:, None, None, None]
    coef_y = stiffness[1][:, None, None, None]
    coef_z = stiffness[2][:, None, None, None]
    coef_xy = cross[:, None, None, None]
    gradient_term = coef_x * second_x + coef_y * second_y + coef_z * second_z + 2.0 * coef_xy * mixed
    force = order_field * order_field * order_field - order_field + 2.0 * order_field * coupling - gradient_term
    drift = current[0][None] * slope_x + current[1][None] * slope_y + current[2][None] * slope_z
    return order_field - step_size * (force + drift)


def reference(noise, labels, pair_class, class_gain, stiffness, cross, current):
    grain_ids = jnp.arange(noise.shape[0], dtype=jnp.int32)
    order_field = seed_level * (labels[None] == grain_ids[:, None, None, None]).astype(jnp.float32) + noise
    pair = pair_matrix(pair_class, class_gain)
    for section_index in range(3):
        squares = (order_field * order_field).astype(jnp.bfloat16)
        coupling = jnp.dot(pair, squares.reshape(squares.shape[0], -1),
                           preferred_element_type=jnp.float32).reshape(order_field.shape)
        wrapped = jnp.pad(order_field, ((0, 0), (0, 0), (1, 1), (1, 1)), mode="wrap")
        padded = jnp.pad(wrapped, ((0, 0), (1, 1), (0, 0), (0, 0)), mode="edge")
        order_field = advance(order_field, padded, coupling, stiffness, cross, current)
    return order_field
```

```python
import functools

import jax
import jax.numpy as jnp
from jax import lax
from jax.experimental import pallas as pl
from jax.experimental.pallas import tpu as pltpu
from jax.sharding import PartitionSpec as P

MESH = pl.DeviceIdType.MESH
seed_level = 0.7

PEERS, LAYERS, CHUNKS, DEPTH = 32, 16, 4, 4
ROWS, COLS = 32, 8
NOISE_TOP = 0.15
IN_SCALE = 32767.0 / NOISE_TOP
CODE_S = 2.0**-10
CODE_K = 32767.0 / 23.0
DIRS = ((0, -1), (0, 1), (-1, 0), (1, 0), (-1, -1), (-1, 1), (1, -1), (1, 1))
RIM_ROWS = (128, 128, 32, 32, 16, 16, 16, 16)
RIM_AT = (0, 128, 256, 288, 320, 336, 352, 368)
RIM_TOTAL = 384
RIM_BASE = (0, 4, 9)
RIM_SLOTS = 14


def exchange_kernel(
    n_gx,
    n_gy,
    noise_hbm,
    labels_hbm,
    class_ref,
    gain_ref,
    stiff_ref,
    cross_ref,
    current_hbm,
    out_hbm,
    noise,
    labels,
    current,
    outv,
    send_in,
    recv_in,
    send_out,
    recv_out,
    plane,
    field,
    drift,
    rim_send,
    rim_recv,
    coef_recv,
    coef_send,
    coef,
    pair_ref,
    load_sem,
    store_sem,
    in_send_sem,
    in_recv_sem,
    out_send_sem,
    out_recv_sem,
    rim_send_sem,
    rim_recv_sem,
    coef_send_sem,
    coef_recv_sem,
):
    gx, gy, ga = lax.axis_index("gx"), lax.axis_index("gy"), lax.axis_index("ga")
    sx, sy = ga // 16, ga % 16

    def neighbour(dx, dy):
        to_gx, to_gy, to_sx, to_sy = gx, gy, sx, sy
        if dx:
            to_sx = 1 - sx
            to_gx = (gx + sx) % n_gx if dx > 0 else (gx + n_gx - 1 + sx) % n_gx
        if dy > 0:
            to_sy = (sy + 1) % 16
            to_gy = (gy + (sy + 1) // 16) % n_gy
        if dy < 0:
            to_sy = (sy + 15) % 16
            to_gy = (gy + n_gy - 1 + (sy + 15) // 16) % n_gy
        return to_gx, to_gy, to_sx * 16 + to_sy

    def peer(k):
        return (gx, gy, (ga + k) % PEERS)

    def noise_load(c):
        at = pl.ds(c * DEPTH, DEPTH)
        return pltpu.make_async_copy(noise_hbm.at[:, at], noise.at[:, at], load_sem.at[c])

    half = pl.ds(pl.multiple_of(sx * ROWS, ROWS), ROWS)
    labels_load = pltpu.make_async_copy(labels_hbm.at[:, half], labels, load_sem.at[4])
    current_load = pltpu.make_async_copy(current_hbm.at[:, :, half], current, load_sem.at[5])
    for c in range(CHUNKS):
        noise_load(c).start()
    labels_load.start()
    current_load.start()

    barrier = pltpu.get_barrier_semaphore()

    def greet(k, _):
        pl.semaphore_signal(barrier, inc=1, device_id=peer(k), device_id_type=MESH)
        return 0

    lax.fori_loop(1, PEERS, greet, 0)
    for dx, dy in DIRS:
        pl.semaphore_signal(barrier, inc=1, device_id=neighbour(dx, dy), device_id_type=MESH)

    lane = lax.broadcasted_iota(jnp.int32, (1, 128), 1)
    rows = []
    for r in range(4):
        row = jnp.zeros((1, 128), jnp.float32)
        for k in range(4):
            value = stiff_ref[r, k] if r < 3 else cross_ref[k]
            row = jnp.where(lane == ga * 4 + k, value, row)
        rows.append(row)
    coef_send[...] = jnp.concatenate(rows + [jnp.zeros((4, 128), jnp.float32)], axis=0)

    def encode_in(c):
        for side in range(2):
            for gp in range(2):
                parts = []
                for g in (2 * gp, 2 * gp + 1):
                    block = noise[g, pl.ds(c * DEPTH, DEPTH), side * ROWS : (side + 1) * ROWS, :]
                    code = jnp.round(block.reshape(128, 128).T * IN_SCALE)
                    parts.append(code.reshape(16, 8, 128))
                both = jnp.concatenate(parts, axis=1).astype(jnp.int32).astype(jnp.int16)
                send_in[c, side * 16 : side * 16 + 16, gp * 16 : gp * 16 + 16, :] = both

    noise_load(0).wait()
    encode_in(0)
    pl.semaphore_wait(barrier, PEERS - 1 + len(DIRS))

    def start_coef(k, _):
        pltpu.make_async_remote_copy(
            coef_send, coef_recv.at[ga], coef_send_sem, coef_recv_sem, device_id=peer(k), device_id_type=MESH
        ).start()
        return 0

    lax.fori_loop(1, PEERS, start_coef, 0)
    pltpu.make_async_copy(coef_send, coef_recv.at[ga], coef_recv_sem).start()

    def start_in(c):
        def one(k, _):
            to = (ga + k) % PEERS
            pltpu.make_async_remote_copy(
                send_in.at[c, to], recv_in.at[c, ga], in_send_sem, in_recv_sem.at[c],
                device_id=(gx, gy, to), device_id_type=MESH,
            ).start()
            return 0

        lax.fori_loop(1, PEERS, one, 0)
        pltpu.make_async_copy(send_in.at[c, ga], recv_in.at[c, ga], in_recv_sem.at[c]).start()

    start_in(0)
    for c in range(1, CHUNKS):
        noise_load(c).wait()
        encode_in(c)
        start_in(c)

    picked = jnp.zeros((128, 128), jnp.float32)
    for k in range(4):
        picked = jnp.where(class_ref[...] == k, gain_ref[k], picked)
    row_id = lax.broadcasted_iota(jnp.int32, (128, 128), 0)
    col_id = lax.broadcasted_iota(jnp.int32, (128, 128), 1)
    symmetric = jnp.where(row_id == col_id, 0.0, 0.5 * (picked + picked.T))
    pair_ref[...] = (symmetric.astype(jnp.bfloat16).astype(jnp.float32) * 2.0).astype(jnp.bfloat16)

    labels_load.wait()
    current_load.wait()
    shift = (128 - sy * COLS) % 128
    grain = lax.broadcasted_iota(jnp.int32, (ROWS, 128), 1)

    def spread(z, _):
        own = pltpu.roll(labels[z], shift, 1)
        for y in range(COLS):
            column = jnp.broadcast_to(own[:, y : y + 1], (ROWS, 128))
            field[0, z * 10 + y + 1, 8:40, :] = jnp.where(column == grain, seed_level, 0.0)
        for k in range(3):
            flow = pltpu.roll(current[k, z] * 0.05, shift, 1)
            for y in range(COLS):
                drift[k, z * COLS + y] = jnp.broadcast_to(flow[:, y : y + 1], (ROWS, 128))
        return 0

    lax.fori_loop(0, LAYERS, spread, 0)

    pltpu.make_async_copy(coef_recv, coef_recv, coef_recv_sem).wait()
    total = jnp.sum(coef_recv[...], axis=0)
    k_x, k_y, k_z, k_xy = (jnp.broadcast_to(total[r : r + 1], (8, 128)) for r in range(4))
    coef[0] = 1.1 - 0.2 * (k_x + k_y + k_z)
    coef[1] = 0.1 * k_x
    coef[2] = 0.1 * k_y
    coef[3] = 0.1 * k_z
    coef[4] = 0.05 * k_xy

    def arrive(c):
        pltpu.make_async_copy(recv_in.at[c], recv_in.at[c], in_recv_sem.at[c]).wait()
        for p in range(0, PEERS, 4):
            block = recv_in[c, p : p + 4].astype(jnp.int32).astype(jnp.float32) * (1.0 / IN_SCALE)
            plane[p * 32 : (p + 4) * 32, :] = block.reshape(128, 128)
        for y in range(COLS):
            block = plane[pl.ds(y, 128, stride=8), :].T
            for d in range(DEPTH):
                at = (c * DEPTH + d) * 10 + y + 1
                field[0, at, 8:40, :] = field[0, at, 8:40, :] + block[d * ROWS : (d + 1) * ROWS]

    def layer_of(c, s, d):
        return jnp.clip(c * DEPTH - s + d, 0, LAYERS - 1)

    def rim_copies(s, c):
        slot = RIM_BASE[s] + c
        for n, (dx, dy) in enumerate(DIRS):
            m = DIRS.index((-dx, -dy))
            yield pltpu.make_async_remote_copy(
                rim_send.at[slot, pl.ds(RIM_AT[n], RIM_ROWS[n])], rim_recv.at[slot, pl.ds(RIM_AT[m], RIM_ROWS[m])],
                rim_send_sem, rim_recv_sem.at[slot], device_id=neighbour(dx, dy), device_id_type=MESH,
            )

    flat = field.reshape(4, LAYERS * 10 * 48, 128)

    def send_rims(s, c):
        slot = RIM_BASE[s] + c
        layers = [layer_of(c, s, d) for d in range(DEPTH)]
        for d, z in enumerate(layers):
            rim_send[slot, d * ROWS : (d + 1) * ROWS, :] = field[s, z * 10 + 1, 8:40, :].astype(jnp.bfloat16)
            rim_send[slot, 128 + d * ROWS : 128 + (d + 1) * ROWS, :] = field[s, z * 10 + 8, 8:40, :].astype(jnp.bfloat16)
        for n, x in ((2, 8), (3, 39)):
            for d in range(0, DEPTH, 2):
                pieces = [flat[s, pl.ds((layers[e] * 10 + 1) * 48 + x, COLS, stride=48), :] for e in (d, d + 1)]
                at = RIM_AT[n] + d * COLS
                rim_send[slot, at : at + 16, :] = jnp.concatenate(pieces, axis=0).astype(jnp.bfloat16)
        for n, (y, x) in ((4, (1, 8)), (5, (8, 8)), (6, (1, 39)), (7, (8, 39))):
            pieces = [field[s, z * 10 + y, x : x + 1, :] for z in layers] + [jnp.zeros((12, 128), jnp.float32)]
            rim_send[slot, RIM_AT[n] : RIM_AT[n] + 16, :] = jnp.concatenate(pieces, axis=0).astype(jnp.bfloat16)
        for copy in rim_copies(s, c):
            copy.start()

    def take_rims(s, c):
        slot = RIM_BASE[s] + c
        pltpu.make_async_copy(rim_recv.at[slot], rim_recv.at[slot], rim_recv_sem.at[slot]).wait()
        layers = [layer_of(c, s, d) for d in range(DEPTH)]
        for d, z in enumerate(layers):
            field[s, z * 10, 8:40, :] = rim_recv[slot, d * ROWS : (d + 1) * ROWS, :].astype(jnp.float32)
            field[s, z * 10 + 9, 8:40, :] = rim_recv[slot, 128 + d * ROWS : 128 + (d + 1) * ROWS, :].astype(jnp.float32)
        for n, x in ((2, 7), (3, 40)):
            for d in range(0, DEPTH, 2):
                at = RIM_AT[n] + d * COLS
                pieces = rim_recv[slot, at : at + 16, :].astype(jnp.float32)
                for e in (0, 1):
                    flat[s, pl.ds((layers[d + e] * 10 + 1) * 48 + x, COLS, stride=48), :] = pieces[e * 8 : e * 8 + 8]
        for n, (y, x) in ((4, (0, 7)), (5, (9, 7)), (6, (0, 40)), (7, (9, 40))):
            pieces = rim_recv[slot, RIM_AT[n] : RIM_AT[n] + 16, :].astype(jnp.float32)
            for d, z in enumerate(layers):
                field[s, z * 10 + y, x : x + 1, :] = pieces[d : d + 1]

    def step(s, c):
        def one(z, _):
            here = z * 10
            above = jnp.minimum(z + 1, LAYERS - 1) * 10
            below = jnp.maximum(z - 1, 0) * 10
            squares = [jnp.square(field[s - 1, here + y + 1, 8:40, :]).astype(jnp.bfloat16) for y in range(COLS)]
            twice = jnp.dot(jnp.concatenate(squares, axis=0), pair_ref[...], preferred_element_type=jnp.float32)

            def wide(n):
                return jnp.concatenate([coef[n]] * 4, axis=0)

            a_0, a_x, a_y, a_z, a_xy = (wide(n) for n in range(5))

            def slope(y):
                return field[s - 1, here + y + 1, 9:41, :] - field[s - 1, here + y + 1, 7:39, :]

            slopes = [slope(-1), slope(0)]
            for y in range(COLS):
                slopes.append(slope(y + 1))
                v = field[s - 1, here + y + 1, 8:40, :]
                x_p, x_m = field[s - 1, here + y + 1, 9:41, :], field[s - 1, here + y + 1, 7:39, :]
                y_p, y_m = field[s - 1, here + y + 2, 8:40, :], field[s - 1, here + y, 8:40, :]
                z_p, z_m = field[s - 1, above + y + 1, 8:40, :], field[s - 1, below + y + 1, 8:40, :]
                new = v * (a_0 - 0.1 * (v * v + twice[y * ROWS : (y + 1) * ROWS]))
                new = new + a_x * (x_p + x_m) + a_y * (y_p + y_m) + a_z * (z_p + z_m)
                new = new + a_xy * (slopes[y + 2] - slopes[y])
                at = z * COLS + y
                new = new - (drift[0, at] * slopes[y + 1] + drift[1, at] * (y_p - y_m) + drift[2, at] * (z_p - z_m))
                field[s, here + y + 1, 8:40, :] = new
            return 0

        first = jnp.maximum(c * DEPTH - s, 0)
        last = jnp.minimum(c * DEPTH - s + DEPTH, LAYERS)
        lax.fori_loop(first, last, one, 0)

    def leave(c):
        for y in range(COLS):
            parts = [field[3, (c * DEPTH + d) * 10 + y + 1, 8:40, :] for d in range(DEPTH)]
            plane[pl.ds(y, 128, stride=8), :] = jnp.concatenate(parts, axis=0).T
        for p in range(0, PEERS, 4):
            block = plane[p * 32 : (p + 4) * 32, :].reshape(4, 32, 128)
            level = jnp.minimum(jnp.round(CODE_K * jnp.log2(1.0 + jnp.abs(block) * (1.0 / CODE_S))), 32767.0)
            code = jnp.where(block < 0.0, -level, level)
            send_out[c, p : p + 4] = code.astype(jnp.int32).astype(jnp.int16)

        def one(k, _):
            to = (ga + k) % PEERS
            pltpu.make_async_remote_copy(
                send_out.at[c, to], recv_out.at[c, ga], out_send_sem, out_recv_sem.at[c],
                device_id=(gx, gy, to), device_id_type=MESH,
            ).start()
            return 0

        lax.fori_loop(1, PEERS, one, 0)
        pltpu.make_async_copy(send_out.at[c, ga], recv_out.at[c, ga], out_recv_sem.at[c]).start()

    def turn(i, _):
        @pl.when(i < CHUNKS)
        def _():
            arrive(i)
            send_rims(0, i)

        @pl.when(i >= 1)
        def _():
            take_rims(1, i - 1)
            step(2, i - 1)
            send_rims(2, i - 1)

        @pl.when(i < CHUNKS)
        def _():
            take_rims(0, i)

        @pl.when(i <= CHUNKS)
        def _():
            step(1, i)
            send_rims(1, i)

        @pl.when(i >= 1)
        def _():
            take_rims(2, i - 1)
            step(3, i - 1)

        @pl.when(i >= 2)
        def _():
            leave(i - 2)

        return 0

    lax.fori_loop(0, CHUNKS + 2, turn, 0)

    def store(c):
        at = pl.ds(c * DEPTH, DEPTH)
        return pltpu.make_async_copy(outv.at[:, at], out_hbm.at[:, at], store_sem.at[c])

    def finish(c, _):
        pltpu.make_async_copy(recv_out.at[c], recv_out.at[c], out_recv_sem.at[c]).wait()
        for side in range(2):
            for gp in range(2):
                code = recv_out[c, side * 16 : side * 16 + 16, gp * 16 : gp * 16 + 16, :]
                level = code.astype(jnp.int32).astype(jnp.float32) * (1.0 / CODE_K)
                size = jnp.exp2(jnp.abs(level)) * CODE_S - CODE_S
                value = jnp.where(level < 0.0, -size, size)
                for e in range(2):
                    block = value[:, e * 8 : e * 8 + 8, :].reshape(128, 128).T
                    outv[2 * gp + e, pl.ds(c * DEPTH, DEPTH), side * ROWS : (side + 1) * ROWS, :] = block.reshape(
                        DEPTH, ROWS, 128
                    )
        store(c).start()
        return 0

    lax.fori_loop(0, CHUNKS, finish, 0)
    for c in range(CHUNKS):
        store(c).wait()
    most = pl.ds(0, PEERS - 1)
    pltpu.make_async_copy(send_in.at[:, most], send_in.at[:, most], in_send_sem).wait()
    pltpu.make_async_copy(send_out.at[:, most], send_out.at[:, most], out_send_sem).wait()
    pltpu.make_async_copy(rim_send, rim_send, rim_send_sem).wait()
    pltpu.make_async_copy(coef_recv.at[most], coef_recv.at[most], coef_send_sem).wait()


def per_device(n_gx, n_gy, noise, labels, pair_class, class_gain, stiffness, cross, current):
    hbm = pl.BlockSpec(memory_space=pl.ANY)
    vmem = pl.BlockSpec(memory_space=pltpu.VMEM)
    smem = pl.BlockSpec(memory_space=pltpu.SMEM)
    dma = pltpu.SemaphoreType.DMA
    f32, bf16, i16 = jnp.float32, jnp.bfloat16, jnp.int16
    return pl.pallas_call(
        functools.partial(exchange_kernel, n_gx, n_gy),
        out_shape=jax.ShapeDtypeStruct(noise.shape, f32),
        in_specs=[hbm, hbm, vmem, smem, smem, smem, hbm],
        out_specs=hbm,
        scratch_shapes=[
            pltpu.VMEM((4, LAYERS, 64, 128), f32),
            pltpu.VMEM((LAYERS, ROWS, 128), jnp.int32),
            pltpu.VMEM((3, LAYERS, ROWS, 128), f32),
            pltpu.VMEM((4, LAYERS, 64, 128), f32),
            pltpu.VMEM((CHUNKS, PEERS, 32, 128), i16),
            pltpu.VMEM((CHUNKS, PEERS, 32, 128), i16),
            pltpu.VMEM((CHUNKS, PEERS, 32, 128), i16),
            pltpu.VMEM((CHUNKS, PEERS, 32, 128), i16),
            pltpu.VMEM((PEERS * 32, 128), f32),
            pltpu.VMEM((4, LAYERS * 10, 48, 128), f32),
            pltpu.VMEM((3, LAYERS * COLS, ROWS, 128), f32),
            pltpu.VMEM((RIM_SLOTS, RIM_TOTAL, 128), bf16),
            pltpu.VMEM((RIM_SLOTS, RIM_TOTAL, 128), bf16),
            pltpu.VMEM((PEERS, 8, 128), f32),
            pltpu.VMEM((8, 128), f32),
            pltpu.VMEM((5, 8, 128), f32),
            pltpu.VMEM((128, 128), bf16),
            dma((6,)),
            dma((CHUNKS,)),
            dma,
            dma((CHUNKS,)),
            dma,
            dma((CHUNKS,)),
            dma,
            dma((RIM_SLOTS,)),
            dma,
            dma,
        ],
        compiler_params=pltpu.CompilerParams(
            collective_id=0, has_side_effects=True, vmem_limit_bytes=60 * 1024 * 1024
        ),
        name="phase_steps",
    )(noise, labels, pair_class, class_gain, stiffness, cross, current)


def solution(mesh):
    placed = (
        P("ga", None, "gx", "gy"),
        P(None, "gx", "gy"),
        P(),
        P(),
        P(None, "ga"),
        P("ga"),
        P(None, None, "gx", "gy"),
    )
    return jax.shard_map(
        functools.partial(per_device, mesh.shape["gx"], mesh.shape["gy"]),
        mesh=mesh,
        in_specs=placed,
        out_specs=P("ga", None, "gx", "gy"),
        check_vma=False,
    )
```

```python
import functools

import jax
import jax.numpy as jnp
from jax import lax
from jax.experimental import pallas as pl
from jax.experimental.pallas import tpu as pltpu
from jax.sharding import PartitionSpec as P

MESH = pl.DeviceIdType.MESH
seed_level = 0.7

PEERS, LAYERS, CHUNKS, DEPTH = 32, 16, 4, 4
ROWS, COLS = 32, 8
NOISE_TOP = 0.15
IN_SCALE = 32767.0 / NOISE_TOP
CODE_S = 2.0**-10
CODE_K = 32767.0 / 23.0
DIRS = ((0, -1), (0, 1), (-1, 0), (1, 0), (-1, -1), (-1, 1), (1, -1), (1, 1))
RIM_ROWS = (128, 128, 32, 32, 16, 16, 16, 16)
RIM_AT = (0, 128, 256, 288, 320, 336, 352, 368)
RIM_TOTAL = 384
RIM_BASE = (0, 4, 9)
RIM_SLOTS = 14


def exchange_kernel(
    n_gx,
    n_gy,
    noise_hbm,
    labels_hbm,
    class_ref,
    gain_ref,
    stiff_ref,
    cross_ref,
    current_hbm,
    out_hbm,
    noise,
    labels,
    current,
    outv,
    send_in,
    recv_in,
    send_out,
    recv_out,
    plane,
    field,
    drift,
    rim_send,
    rim_recv,
    coef_recv,
    coef_send,
    coef,
    pair_ref,
    load_sem,
    store_sem,
    in_send_sem,
    in_recv_sem,
    out_send_sem,
    out_recv_sem,
    rim_send_sem,
    rim_recv_sem,
    coef_send_sem,
    coef_recv_sem,
):
    gx, gy, ga = lax.axis_index("gx"), lax.axis_index("gy"), lax.axis_index("ga")
    sx, sy = ga // 16, ga % 16

    def neighbour(dx, dy):
        to_gx, to_gy, to_sx, to_sy = gx, gy, sx, sy
        if dx:
            to_sx = 1 - sx
            to_gx = (gx + sx) % n_gx if dx > 0 else (gx + n_gx - 1 + sx) % n_gx
        if dy > 0:
            to_sy = (sy + 1) % 16
            to_gy = (gy + (sy + 1) // 16) % n_gy
        if dy < 0:
            to_sy = (sy + 15) % 16
            to_gy = (gy + n_gy - 1 + (sy + 15) // 16) % n_gy
        return to_gx, to_gy, to_sx * 16 + to_sy

    def peer(k):
        return (gx, gy, (ga + k) % PEERS)

    def noise_load(c):
        at = pl.ds(c * DEPTH, DEPTH)
        return pltpu.make_async_copy(noise_hbm.at[:, at], noise.at[:, at], load_sem.at[c])

    half = pl.ds(pl.multiple_of(sx * ROWS, ROWS), ROWS)
    labels_load = pltpu.make_async_copy(labels_hbm.at[:, half], labels, load_sem.at[4])
    current_load = pltpu.make_async_copy(current_hbm.at[:, :, half], current, load_sem.at[5])
    for c in range(CHUNKS):
        noise_load(c).start()
    labels_load.start()
    current_load.start()

    barrier = pltpu.get_barrier_semaphore()

    def greet(k, _):
        pl.semaphore_signal(barrier, inc=1, device_id=peer(k), device_id_type=MESH)
        return 0

    lax.fori_loop(1, PEERS, greet, 0)
    for dx, dy in DIRS:
        pl.semaphore_signal(barrier, inc=1, device_id=neighbour(dx, dy), device_id_type=MESH)

    lane = lax.broadcasted_iota(jnp.int32, (1, 128), 1)
    rows = []
    for r in range(4):
        row = jnp.zeros((1, 128), jnp.float32)
        for k in range(4):
            value = stiff_ref[r, k] if r < 3 else cross_ref[k]
            row = jnp.where(lane == ga * 4 + k, value, row)
        rows.append(row)
    coef_send[0] = jnp.concatenate(rows + [jnp.zeros((4, 128), jnp.float32)], axis=0)

    def encode_in(c):
        for side in range(2):
            for gp in range(2):
                parts = []
                for g in (2 * gp, 2 * gp + 1):
                    block = noise[g, pl.ds(c * DEPTH, DEPTH), side * ROWS : (side + 1) * ROWS, :]
                    code = jnp.round(block.reshape(128, 128).T * IN_SCALE)
                    parts.append(code.reshape(16, 8, 128))
                both = jnp.concatenate(parts, axis=1).astype(jnp.int32).astype(jnp.int16)
                send_in[c, side * 16 : side * 16 + 16, gp * 16 : gp * 16 + 16, :] = both

    noise_load(0).wait()
    encode_in(0)
    pl.semaphore_wait(barrier, PEERS - 1 + len(DIRS))

    chip = sy // 2

    def coef_first(k):
        to = sx * 16 + ((chip + k) % 8) * 2 + sy % 2
        return pltpu.make_async_remote_copy(
            coef_send.at[0], coef_recv.at[0, chip], coef_send_sem.at[0], coef_recv_sem.at[0],
            device_id=(gx, gy, to), device_id_type=MESH,
        )

    group = sx * 2 + sy % 2

    def coef_second(k):
        to = (group + k) % 4
        return pltpu.make_async_remote_copy(
            coef_send.at[1], coef_recv.at[1, group], coef_send_sem.at[1], coef_recv_sem.at[1],
            device_id=(gx, gy, (to // 2) * 16 + chip * 2 + to % 2), device_id_type=MESH,
        )

    for k in range(1, 8):
        coef_first(k).start()
    pltpu.make_async_copy(coef_send.at[0], coef_recv.at[0, chip], coef_recv_sem.at[0]).start()

    def swap(send, recv, send_sem, recv_sem, c):
        def one(k, _):
            to = (ga + k) % PEERS
            pltpu.make_async_remote_copy(
                send.at[c, to], recv.at[c, ga], send_sem, recv_sem.at[c],
                device_id=(gx, gy, to), device_id_type=MESH,
            ).start()
            return 0

        lax.fori_loop(1, PEERS, one, 0)
        pltpu.make_async_copy(send.at[c, ga], recv.at[c, ga], recv_sem.at[c]).start()

    swap(send_in, recv_in, in_send_sem, in_recv_sem, 0)
    for c in range(1, CHUNKS):
        noise_load(c).wait()
        encode_in(c)
        swap(send_in, recv_in, in_send_sem, in_recv_sem, c)

    picked = jnp.zeros((128, 128), jnp.float32)
    for k in range(4):
        picked = jnp.where(class_ref[...] == k, gain_ref[k], picked)
    row_id = lax.broadcasted_iota(jnp.int32, (128, 128), 0)
    col_id = lax.broadcasted_iota(jnp.int32, (128, 128), 1)
    symmetric = jnp.where(row_id == col_id, 0.0, 0.5 * (picked + picked.T))
    pair_ref[...] = (symmetric.astype(jnp.bfloat16).astype(jnp.float32) * 2.0).astype(jnp.bfloat16)

    labels_load.wait()
    current_load.wait()
    shift = (128 - sy * COLS) % 128
    grain = lax.broadcasted_iota(jnp.int32, (ROWS, 128), 1)

    def spread(z, _):
        own = pltpu.roll(labels[z], shift, 1)
        for y in range(COLS):
            column = jnp.broadcast_to(own[:, y : y + 1], (ROWS, 128))
            field[0, z * 10 + y + 1, 8:40, :] = jnp.where(column == grain, seed_level, 0.0)
        for k in range(3):
            flow = pltpu.roll(current[k, z] * 0.05, shift, 1)
            for y in range(COLS):
                drift[k, z * COLS + y] = jnp.broadcast_to(flow[:, y : y + 1], (ROWS, 128))
        return 0

    pltpu.make_async_copy(coef_recv.at[0], coef_recv.at[0], coef_recv_sem.at[0]).wait()
    coef_send[1] = jnp.sum(coef_recv[0], axis=0)
    for k in range(1, 4):
        coef_second(k).start()
    pltpu.make_async_copy(coef_send.at[1], coef_recv.at[1, group], coef_recv_sem.at[1]).start()

    lax.fori_loop(0, LAYERS, spread, 0)

    quarter = coef_recv.at[1, pl.ds(0, 4)]
    pltpu.make_async_copy(quarter, quarter, coef_recv_sem.at[1]).wait()
    total = jnp.sum(coef_recv[1, 0:4], axis=0)
    k_x, k_y, k_z, k_xy = (jnp.broadcast_to(total[r : r + 1], (8, 128)) for r in range(4))
    coef[0] = 1.1 - 0.2 * (k_x + k_y + k_z)
    coef[1] = 0.1 * k_x
    coef[2] = 0.1 * k_y
    coef[3] = 0.1 * k_z
    coef[4] = 0.05 * k_xy

    def arrive(c):
        pltpu.make_async_copy(recv_in.at[c], recv_in.at[c], in_recv_sem.at[c]).wait()
        for p in range(0, PEERS, 4):
            block = recv_in[c, p : p + 4].astype(jnp.int32).astype(jnp.float32) * (1.0 / IN_SCALE)
            plane[p * 32 : (p + 4) * 32, :] = block.reshape(128, 128)
        for y in range(COLS):
            block = plane[pl.ds(y, 128, stride=8), :].T
            for d in range(DEPTH):
                at = (c * DEPTH + d) * 10 + y + 1
                field[0, at, 8:40, :] = field[0, at, 8:40, :] + block[d * ROWS : (d + 1) * ROWS]

    def layer_of(c, s, d):
        return jnp.clip(c * DEPTH - s + d, 0, LAYERS - 1)

    def rim_copies(s, c):
        slot = RIM_BASE[s] + c
        for n, (dx, dy) in enumerate(DIRS):
            m = DIRS.index((-dx, -dy))
            yield pltpu.make_async_remote_copy(
                rim_send.at[slot, pl.ds(RIM_AT[n], RIM_ROWS[n])], rim_recv.at[slot, pl.ds(RIM_AT[m], RIM_ROWS[m])],
                rim_send_sem, rim_recv_sem.at[slot], device_id=neighbour(dx, dy), device_id_type=MESH,
            )

    flat = field.reshape(4, LAYERS * 10 * 48, 128)

    def send_rims(s, c):
        slot = RIM_BASE[s] + c
        layers = [layer_of(c, s, d) for d in range(DEPTH)]
        for d, z in enumerate(layers):
            rim_send[slot, d * ROWS : (d + 1) * ROWS, :] = field[s, z * 10 + 1, 8:40, :].astype(jnp.bfloat16)
            rim_send[slot, 128 + d * ROWS : 128 + (d + 1) * ROWS, :] = field[s, z * 10 + 8, 8:40, :].astype(jnp.bfloat16)
        for n, x in ((2, 8), (3, 39)):
            for d in range(0, DEPTH, 2):
                pieces = [flat[s, pl.ds((layers[e] * 10 + 1) * 48 + x, COLS, stride=48), :] for e in (d, d + 1)]
                at = RIM_AT[n] + d * COLS
                rim_send[slot, at : at + 16, :] = jnp.concatenate(pieces, axis=0).astype(jnp.bfloat16)
        for n, (y, x) in ((4, (1, 8)), (5, (8, 8)), (6, (1, 39)), (7, (8, 39))):
            pieces = [field[s, z * 10 + y, x : x + 1, :] for z in layers] + [jnp.zeros((12, 128), jnp.float32)]
            rim_send[slot, RIM_AT[n] : RIM_AT[n] + 16, :] = jnp.concatenate(pieces, axis=0).astype(jnp.bfloat16)
        for copy in rim_copies(s, c):
            copy.start()

    def take_rims(s, c):
        slot = RIM_BASE[s] + c
        pltpu.make_async_copy(rim_recv.at[slot], rim_recv.at[slot], rim_recv_sem.at[slot]).wait()
        layers = [layer_of(c, s, d) for d in range(DEPTH)]
        for d, z in enumerate(layers):
            field[s, z * 10, 8:40, :] = rim_recv[slot, d * ROWS : (d + 1) * ROWS, :].astype(jnp.float32)
            field[s, z * 10 + 9, 8:40, :] = rim_recv[slot, 128 + d * ROWS : 128 + (d + 1) * ROWS, :].astype(jnp.float32)
        for n, x in ((2, 7), (3, 40)):
            for d in range(0, DEPTH, 2):
                at = RIM_AT[n] + d * COLS
                pieces = rim_recv[slot, at : at + 16, :].astype(jnp.float32)
                for e in (0, 1):
                    flat[s, pl.ds((layers[d + e] * 10 + 1) * 48 + x, COLS, stride=48), :] = pieces[e * 8 : e * 8 + 8]
        for n, (y, x) in ((4, (0, 7)), (5, (9, 7)), (6, (0, 40)), (7, (9, 40))):
            pieces = rim_recv[slot, RIM_AT[n] : RIM_AT[n] + 16, :].astype(jnp.float32)
            for d, z in enumerate(layers):
                field[s, z * 10 + y, x : x + 1, :] = pieces[d : d + 1]

    def step(s, c):
        def one(z, _):
            here = z * 10
            above = jnp.minimum(z + 1, LAYERS - 1) * 10
            below = jnp.maximum(z - 1, 0) * 10
            squares = [jnp.square(field[s - 1, here + y + 1, 8:40, :]).astype(jnp.bfloat16) for y in range(COLS)]
            twice = jnp.dot(jnp.concatenate(squares, axis=0), pair_ref[...], preferred_element_type=jnp.float32)

            def wide(n):
                return jnp.concatenate([coef[n]] * 4, axis=0)

            a_0, a_x, a_y, a_z, a_xy = (wide(n) for n in range(5))

            def slope(y):
                return field[s - 1, here + y + 1, 9:41, :] - field[s - 1, here + y + 1, 7:39, :]

            slopes = [slope(-1), slope(0)]
            for y in range(COLS):
                slopes.append(slope(y + 1))
                v = field[s - 1, here + y + 1, 8:40, :]
                x_p, x_m = field[s - 1, here + y + 1, 9:41, :], field[s - 1, here + y + 1, 7:39, :]
                y_p, y_m = field[s - 1, here + y + 2, 8:40, :], field[s - 1, here + y, 8:40, :]
                z_p, z_m = field[s - 1, above + y + 1, 8:40, :], field[s - 1, below + y + 1, 8:40, :]
                new = v * (a_0 - 0.1 * (v * v + twice[y * ROWS : (y + 1) * ROWS]))
                new = new + a_x * (x_p + x_m) + a_y * (y_p + y_m) + a_z * (z_p + z_m)
                new = new + a_xy * (slopes[y + 2] - slopes[y])
                at = z * COLS + y
                new = new - (drift[0, at] * slopes[y + 1] + drift[1, at] * (y_p - y_m) + drift[2, at] * (z_p - z_m))
                field[s, here + y + 1, 8:40, :] = new
            return 0

        first = jnp.maximum(c * DEPTH - s, 0)
        last = jnp.minimum(c * DEPTH - s + DEPTH, LAYERS)
        lax.fori_loop(first, last, one, 0)

    def leave(c):
        for y in range(COLS):
            parts = [field[3, (c * DEPTH + d) * 10 + y + 1, 8:40, :] for d in range(DEPTH)]
            plane[pl.ds(y, 128, stride=8), :] = jnp.concatenate(parts, axis=0).T
        for p in range(0, PEERS, 4):
            block = plane[p * 32 : (p + 4) * 32, :].reshape(4, 32, 128)
            level = jnp.minimum(jnp.round(CODE_K * jnp.log2(1.0 + jnp.abs(block) * (1.0 / CODE_S))), 32767.0)
            code = jnp.where(block < 0.0, -level, level)
            send_out[c, p : p + 4] = code.astype(jnp.int32).astype(jnp.int16)

    def start(c, _):
        arrive(c)
        send_rims(0, c)
        return 0

    lax.fori_loop(0, CHUNKS, start, 0)

    def first(c, _):
        @pl.when(c < CHUNKS)
        def _():
            take_rims(0, c)

        step(1, c)
        send_rims(1, c)
        return 0

    def second(c, _):
        take_rims(1, c)
        step(2, c)
        send_rims(2, c)
        return 0

    def third(c, _):
        take_rims(2, c)
        step(3, c)

        @pl.when(c >= 1)
        def _():
            leave(c - 1)
            swap(send_out, recv_out, out_send_sem, out_recv_sem, c - 1)

        return 0

    for phase in (first, second, third):
        lax.fori_loop(0, CHUNKS + 1, phase, 0)

    def store(c):
        at = pl.ds(c * DEPTH, DEPTH)
        return pltpu.make_async_copy(outv.at[:, at], out_hbm.at[:, at], store_sem.at[c])

    def finish(c, _):
        pltpu.make_async_copy(recv_out.at[c], recv_out.at[c], out_recv_sem.at[c]).wait()
        for side in range(2):
            for gp in range(2):
                code = recv_out[c, side * 16 : side * 16 + 16, gp * 16 : gp * 16 + 16, :]
                level = code.astype(jnp.int32).astype(jnp.float32)
                for e in range(2):
                    block = level[:, e * 8 : e * 8 + 8, :].reshape(128, 128).T.astype(jnp.int32).astype(jnp.int16)
                    outv[2 * gp + e, pl.ds(c * DEPTH, DEPTH), side * ROWS : (side + 1) * ROWS, :] = block.reshape(
                        DEPTH, ROWS, 128
                    )
        store(c).start()
        return 0

    lax.fori_loop(0, CHUNKS, finish, 0)
    for c in range(CHUNKS):
        store(c).wait()
    most = pl.ds(0, PEERS - 1)
    pltpu.make_async_copy(send_in.at[:, most], send_in.at[:, most], in_send_sem).wait()
    pltpu.make_async_copy(send_out.at[:, most], send_out.at[:, most], out_send_sem).wait()
    pltpu.make_async_copy(rim_send, rim_send, rim_send_sem).wait()
    for n, count in ((0, 7), (1, 3)):
        sent = coef_recv.at[0, pl.ds(0, count)]
        pltpu.make_async_copy(sent, sent, coef_send_sem.at[n]).wait()


def per_device(n_gx, n_gy, noise, labels, pair_class, class_gain, stiffness, cross, current):
    hbm = pl.BlockSpec(memory_space=pl.ANY)
    vmem = pl.BlockSpec(memory_space=pltpu.VMEM)
    smem = pl.BlockSpec(memory_space=pltpu.SMEM)
    dma = pltpu.SemaphoreType.DMA
    f32, bf16, i16 = jnp.float32, jnp.bfloat16, jnp.int16
    code = pl.pallas_call(
        functools.partial(exchange_kernel, n_gx, n_gy),
        out_shape=jax.ShapeDtypeStruct(noise.shape, i16),
        in_specs=[hbm, hbm, vmem, smem, smem, smem, hbm],
        out_specs=hbm,
        scratch_shapes=[
            pltpu.VMEM((4, LAYERS, 64, 128), f32),
            pltpu.VMEM((LAYERS, ROWS, 128), jnp.int32),
            pltpu.VMEM((3, LAYERS, ROWS, 128), f32),
            pltpu.VMEM((4, LAYERS, 64, 128), i16),
            pltpu.VMEM((CHUNKS, PEERS, 32, 128), i16),
            pltpu.VMEM((CHUNKS, PEERS, 32, 128), i16),
            pltpu.VMEM((CHUNKS, PEERS, 32, 128), i16),
            pltpu.VMEM((CHUNKS, PEERS, 32, 128), i16),
            pltpu.VMEM((PEERS * 32, 128), f32),
            pltpu.VMEM((4, LAYERS * 10, 48, 128), f32),
            pltpu.VMEM((3, LAYERS * COLS, ROWS, 128), f32),
            pltpu.VMEM((RIM_SLOTS, RIM_TOTAL, 128), bf16),
            pltpu.VMEM((RIM_SLOTS, RIM_TOTAL, 128), bf16),
            pltpu.VMEM((2, 8, 8, 128), f32),
            pltpu.VMEM((2, 8, 128), f32),
            pltpu.VMEM((5, 8, 128), f32),
            pltpu.VMEM((128, 128), bf16),
            dma((6,)),
            dma((CHUNKS,)),
            dma,
            dma((CHUNKS,)),
            dma,
            dma((CHUNKS,)),
            dma,
            dma((RIM_SLOTS,)),
            dma((2,)),
            dma((2,)),
        ],
        compiler_params=pltpu.CompilerParams(
            collective_id=0, has_side_effects=True, vmem_limit_bytes=60 * 1024 * 1024
        ),
        name="phase_steps",
    )(noise, labels, pair_class, class_gain, stiffness, cross, current)
    level = code.astype(f32) * (1.0 / CODE_K)
    size = jnp.exp2(jnp.abs(level)) * CODE_S - CODE_S
    return jnp.where(level < 0.0, -size, size)


def solution(mesh):
    placed = (
        P("ga", None, "gx", "gy"),
        P(None, "gx", "gy"),
        P(),
        P(),
        P(None, "ga"),
        P("ga"),
        P(None, None, "gx", "gy"),
    )
    return jax.shard_map(
        functools.partial(per_device, mesh.shape["gx"], mesh.shape["gy"]),
        mesh=mesh,
        in_specs=placed,
        out_specs=P("ga", None, "gx", "gy"),
        check_vma=False,
    )
```

```python
import functools

import jax
import jax.numpy as jnp
from jax import lax
from jax.experimental import pallas as pl
from jax.experimental.pallas import tpu as pltpu
from jax.sharding import PartitionSpec as P

MESH = pl.DeviceIdType.MESH
seed_level = 0.7

PEERS, LAYERS, CHUNKS, DEPTH = 32, 16, 4, 4
ROWS, COLS = 32, 8
NOISE_TOP = 0.15
IN_SCALE = 32767.0 / NOISE_TOP
CODE_S = 2.0**-10
CODE_K = 32767.0 / 23.0
DIRS = ((0, -1), (0, 1), (-1, 0), (1, 0), (-1, -1), (-1, 1), (1, -1), (1, 1))
RIM_ROWS = (128, 128, 32, 32, 16, 16, 16, 16)
RIM_AT = (0, 128, 256, 288, 320, 336, 352, 368)
RIM_TOTAL = 384
RIM_BASE = (0, 4, 9)
RIM_SLOTS = 14


def exchange_kernel(
    n_gx,
    n_gy,
    noise_hbm,
    labels_hbm,
    class_hbm,
    gain_hbm,
    stiff_hbm,
    cross_hbm,
    current_hbm,
    out_hbm,
    noise,
    labels,
    current,
    class_ref,
    gain_ref,
    stiff_ref,
    cross_ref,
    outv,
    send_in,
    recv_in,
    send_out,
    recv_out,
    plane,
    field,
    drift,
    rim_send,
    rim_recv,
    coef_recv,
    coef_send,
    coef,
    pair_ref,
    load_sem,
    store_sem,
    in_send_sem,
    in_recv_sem,
    out_send_sem,
    out_recv_sem,
    rim_send_sem,
    rim_recv_sem,
    coef_send_sem,
    coef_recv_sem,
):
    gx, gy, ga = lax.axis_index("gx"), lax.axis_index("gy"), lax.axis_index("ga")
    sx, sy = ga // 16, ga % 16

    def neighbour(dx, dy):
        to_gx, to_gy, to_sx, to_sy = gx, gy, sx, sy
        if dx:
            to_sx = 1 - sx
            to_gx = (gx + sx) % n_gx if dx > 0 else (gx + n_gx - 1 + sx) % n_gx
        if dy > 0:
            to_sy = (sy + 1) % 16
            to_gy = (gy + (sy + 1) // 16) % n_gy
        if dy < 0:
            to_sy = (sy + 15) % 16
            to_gy = (gy + n_gy - 1 + (sy + 15) // 16) % n_gy
        return to_gx, to_gy, to_sx * 16 + to_sy

    def peer(k):
        return (gx, gy, (ga + k) % PEERS)

    def noise_load(c):
        at = pl.ds(c * DEPTH, DEPTH)
        return pltpu.make_async_copy(noise_hbm.at[:, at], noise.at[:, at], load_sem.at[c])

    half = pl.ds(pl.multiple_of(sx * ROWS, ROWS), ROWS)
    labels_load = pltpu.make_async_copy(labels_hbm.at[:, half], labels, load_sem.at[4])
    current_load = pltpu.make_async_copy(current_hbm.at[:, :, half], current, load_sem.at[5])
    small = ((stiff_hbm, stiff_ref), (cross_hbm, cross_ref), (gain_hbm, gain_ref), (class_hbm, class_ref))
    small_loads = [pltpu.make_async_copy(a, b, load_sem.at[6 + n]) for n, (a, b) in enumerate(small)]
    noise_load(0).start()
    for load in small_loads:
        load.start()
    for c in range(1, CHUNKS):
        noise_load(c).start()
    labels_load.start()
    current_load.start()

    barrier = pltpu.get_barrier_semaphore()

    def greet(k, _):
        pl.semaphore_signal(barrier, inc=1, device_id=peer(k), device_id_type=MESH)
        return 0

    lax.fori_loop(1, PEERS, greet, 0)
    for dx, dy in DIRS:
        pl.semaphore_signal(barrier, inc=1, device_id=neighbour(dx, dy), device_id_type=MESH)

    small_loads[0].wait()
    small_loads[1].wait()
    lane = lax.broadcasted_iota(jnp.int32, (1, 128), 1)
    rows = []
    for r in range(4):
        row = jnp.zeros((1, 128), jnp.float32)
        for k in range(4):
            value = stiff_ref[r, k] if r < 3 else cross_ref[k]
            row = jnp.where(lane == ga * 4 + k, value, row)
        rows.append(row)
    coef_send[0] = jnp.concatenate(rows + [jnp.zeros((4, 128), jnp.float32)], axis=0)

    def encode_in(c):
        for side in range(2):
            for gp in range(2):
                parts = []
                for g in (2 * gp, 2 * gp + 1):
                    block = noise[g, pl.ds(c * DEPTH, DEPTH), side * ROWS : (side + 1) * ROWS, :]
                    code = jnp.round(block.reshape(128, 128).T * IN_SCALE)
                    parts.append(code.reshape(16, 8, 128))
                both = jnp.concatenate(parts, axis=1).astype(jnp.int32).astype(jnp.int16)
                send_in[c, side * 16 : side * 16 + 16, gp * 16 : gp * 16 + 16, :] = both

    noise_load(0).wait()
    encode_in(0)
    pl.semaphore_wait(barrier, PEERS - 1 + len(DIRS))

    chip = sy // 2

    def coef_first(k):
        to = sx * 16 + ((chip + k) % 8) * 2 + sy % 2
        return pltpu.make_async_remote_copy(
            coef_send.at[0], coef_recv.at[0, chip], coef_send_sem.at[0], coef_recv_sem.at[0],
            device_id=(gx, gy, to), device_id_type=MESH,
        )

    group = sx * 2 + sy % 2

    def coef_second(k):
        to = (group + k) % 4
        return pltpu.make_async_remote_copy(
            coef_send.at[1], coef_recv.at[1, group], coef_send_sem.at[1], coef_recv_sem.at[1],
            device_id=(gx, gy, (to // 2) * 16 + chip * 2 + to % 2), device_id_type=MESH,
        )

    for k in range(1, 8):
        coef_first(k).start()
    pltpu.make_async_copy(coef_send.at[0], coef_recv.at[0, chip], coef_recv_sem.at[0]).start()

    def swap(send, recv, send_sem, recv_sem, c):
        def one(k, _):
            to = (ga + k) % PEERS
            pltpu.make_async_remote_copy(
                send.at[c, to], recv.at[c, ga], send_sem, recv_sem.at[c],
                device_id=(gx, gy, to), device_id_type=MESH,
            ).start()
            return 0

        lax.fori_loop(1, PEERS, one, 0)
        pltpu.make_async_copy(send.at[c, ga], recv.at[c, ga], recv_sem.at[c]).start()

    swap(send_in, recv_in, in_send_sem, in_recv_sem, 0)
    for c in range(1, CHUNKS):
        noise_load(c).wait()
        encode_in(c)
        if c < CHUNKS - 1:
            swap(send_in, recv_in, in_send_sem, in_recv_sem, c)

    small_loads[2].wait()
    small_loads[3].wait()
    picked = jnp.zeros((128, 128), jnp.float32)
    for k in range(4):
        picked = jnp.where(class_ref[...] == k, gain_ref[k], picked)
    row_id = lax.broadcasted_iota(jnp.int32, (128, 128), 0)
    col_id = lax.broadcasted_iota(jnp.int32, (128, 128), 1)
    symmetric = jnp.where(row_id == col_id, 0.0, 0.5 * (picked + picked.T))
    pair_ref[...] = (symmetric.astype(jnp.bfloat16).astype(jnp.float32) * 2.0).astype(jnp.bfloat16)

    labels_load.wait()
    current_load.wait()
    shift = (128 - sy * COLS) % 128
    grain = lax.broadcasted_iota(jnp.int32, (ROWS, 128), 1)

    def spread(z, _):
        own = pltpu.roll(labels[z], shift, 1)
        for y in range(COLS):
            column = jnp.broadcast_to(own[:, y : y + 1], (ROWS, 128))
            field[0, z * 10 + y + 1, 8:40, :] = jnp.where(column == grain, seed_level, 0.0)
        for k in range(3):
            flow = pltpu.roll(current[k, z] * 0.05, shift, 1)
            for y in range(COLS):
                drift[k, z * COLS + y] = jnp.broadcast_to(flow[:, y : y + 1], (ROWS, 128))
        return 0

    pltpu.make_async_copy(coef_recv.at[0], coef_recv.at[0], coef_recv_sem.at[0]).wait()
    coef_send[1] = jnp.sum(coef_recv[0], axis=0)
    for k in range(1, 4):
        coef_second(k).start()
    pltpu.make_async_copy(coef_send.at[1], coef_recv.at[1, group], coef_recv_sem.at[1]).start()

    lax.fori_loop(0, LAYERS, spread, 0)

    quarter = coef_recv.at[1, pl.ds(0, 4)]
    pltpu.make_async_copy(quarter, quarter, coef_recv_sem.at[1]).wait()
    total = jnp.sum(coef_recv[1, 0:4], axis=0)
    k_x, k_y, k_z, k_xy = (jnp.broadcast_to(total[r : r + 1], (8, 128)) for r in range(4))
    coef[0] = 1.1 - 0.2 * (k_x + k_y + k_z)
    coef[1] = 0.1 * k_x
    coef[2] = 0.1 * k_y
    coef[3] = 0.1 * k_z
    coef[4] = 0.05 * k_xy

    def arrive(c):
        pltpu.make_async_copy(recv_in.at[c], recv_in.at[c], in_recv_sem.at[c]).wait()
        for p in range(0, PEERS, 4):
            block = recv_in[c, p : p + 4].astype(jnp.int32).astype(jnp.float32) * (1.0 / IN_SCALE)
            plane[p * 32 : (p + 4) * 32, :] = block.reshape(128, 128)
        for y in range(COLS):
            block = plane[pl.ds(y, 128, stride=8), :].T
            for d in range(DEPTH):
                at = (c * DEPTH + d) * 10 + y + 1
                field[0, at, 8:40, :] = field[0, at, 8:40, :] + block[d * ROWS : (d + 1) * ROWS]

    def layer_of(c, s, d):
        return jnp.clip(c * DEPTH - s + d, 0, LAYERS - 1)

    def rim_copies(s, c):
        slot = RIM_BASE[s] + c
        for n, (dx, dy) in enumerate(DIRS):
            m = DIRS.index((-dx, -dy))
            yield pltpu.make_async_remote_copy(
                rim_send.at[slot, pl.ds(RIM_AT[n], RIM_ROWS[n])], rim_recv.at[slot, pl.ds(RIM_AT[m], RIM_ROWS[m])],
                rim_send_sem, rim_recv_sem.at[slot], device_id=neighbour(dx, dy), device_id_type=MESH,
            )

    flat = field.reshape(4, LAYERS * 10 * 48, 128)

    def send_rims(s, c):
        slot = RIM_BASE[s] + c
        layers = [layer_of(c, s, d) for d in range(DEPTH)]
        for d, z in enumerate(layers):
            rim_send[slot, d * ROWS : (d + 1) * ROWS, :] = field[s, z * 10 + 1, 8:40, :].astype(jnp.bfloat16)
            rim_send[slot, 128 + d * ROWS : 128 + (d + 1) * ROWS, :] = field[s, z * 10 + 8, 8:40, :].astype(jnp.bfloat16)
        for n, x in ((2, 8), (3, 39)):
            for d in range(0, DEPTH, 2):
                pieces = [flat[s, pl.ds((layers[e] * 10 + 1) * 48 + x, COLS, stride=48), :] for e in (d, d + 1)]
                at = RIM_AT[n] + d * COLS
                rim_send[slot, at : at + 16, :] = jnp.concatenate(pieces, axis=0).astype(jnp.bfloat16)
        for n, (y, x) in ((4, (1, 8)), (5, (8, 8)), (6, (1, 39)), (7, (8, 39))):
            pieces = [field[s, z * 10 + y, x : x + 1, :] for z in layers] + [jnp.zeros((12, 128), jnp.float32)]
            rim_send[slot, RIM_AT[n] : RIM_AT[n] + 16, :] = jnp.concatenate(pieces, axis=0).astype(jnp.bfloat16)
        for copy in rim_copies(s, c):
            copy.start()

    def take_rims(s, c):
        slot = RIM_BASE[s] + c
        pltpu.make_async_copy(rim_recv.at[slot], rim_recv.at[slot], rim_recv_sem.at[slot]).wait()
        layers = [layer_of(c, s, d) for d in range(DEPTH)]
        for d, z in enumerate(layers):
            field[s, z * 10, 8:40, :] = rim_recv[slot, d * ROWS : (d + 1) * ROWS, :].astype(jnp.float32)
            field[s, z * 10 + 9, 8:40, :] = rim_recv[slot, 128 + d * ROWS : 128 + (d + 1) * ROWS, :].astype(jnp.float32)
        for n, x in ((2, 7), (3, 40)):
            for d in range(0, DEPTH, 2):
                at = RIM_AT[n] + d * COLS
                pieces = rim_recv[slot, at : at + 16, :].astype(jnp.float32)
                for e in (0, 1):
                    flat[s, pl.ds((layers[d + e] * 10 + 1) * 48 + x, COLS, stride=48), :] = pieces[e * 8 : e * 8 + 8]
        for n, (y, x) in ((4, (0, 7)), (5, (9, 7)), (6, (0, 40)), (7, (9, 40))):
            pieces = rim_recv[slot, RIM_AT[n] : RIM_AT[n] + 16, :].astype(jnp.float32)
            for d, z in enumerate(layers):
                field[s, z * 10 + y, x : x + 1, :] = pieces[d : d + 1]

    def step(s, c):
        def one(z, _):
            here = z * 10
            above = jnp.minimum(z + 1, LAYERS - 1) * 10
            below = jnp.maximum(z - 1, 0) * 10
            squares = [jnp.square(field[s - 1, here + y + 1, 8:40, :]).astype(jnp.bfloat16) for y in range(COLS)]
            twice = jnp.dot(jnp.concatenate(squares, axis=0), pair_ref[...], preferred_element_type=jnp.float32)

            def wide(n):
                return jnp.concatenate([coef[n]] * 4, axis=0)

            a_0, a_x, a_y, a_z, a_xy = (wide(n) for n in range(5))

            def slope(y):
                return field[s - 1, here + y + 1, 9:41, :] - field[s - 1, here + y + 1, 7:39, :]

            slopes = [slope(-1), slope(0)]
            for y in range(COLS):
                slopes.append(slope(y + 1))
                v = field[s - 1, here + y + 1, 8:40, :]
                x_p, x_m = field[s - 1, here + y + 1, 9:41, :], field[s - 1, here + y + 1, 7:39, :]
                y_p, y_m = field[s - 1, here + y + 2, 8:40, :], field[s - 1, here + y, 8:40, :]
                z_p, z_m = field[s - 1, above + y + 1, 8:40, :], field[s - 1, below + y + 1, 8:40, :]
                new = v * (a_0 - 0.1 * (v * v + twice[y * ROWS : (y + 1) * ROWS]))
                new = new + a_x * (x_p + x_m) + a_y * (y_p + y_m) + a_z * (z_p + z_m)
                new = new + a_xy * (slopes[y + 2] - slopes[y])
                at = z * COLS + y
                new = new - (drift[0, at] * slopes[y + 1] + drift[1, at] * (y_p - y_m) + drift[2, at] * (z_p - z_m))
                field[s, here + y + 1, 8:40, :] = new
            return 0

        first = jnp.maximum(c * DEPTH - s, 0)
        last = jnp.minimum(c * DEPTH - s + DEPTH, LAYERS)
        lax.fori_loop(first, last, one, 0)

    def leave(c):
        for y in range(COLS):
            parts = [field[3, (c * DEPTH + d) * 10 + y + 1, 8:40, :] for d in range(DEPTH)]
            plane[pl.ds(y, 128, stride=8), :] = jnp.concatenate(parts, axis=0).T
        for p in range(0, PEERS, 4):
            block = plane[p * 32 : (p + 4) * 32, :].reshape(4, 32, 128)
            level = jnp.minimum(jnp.round(CODE_K * jnp.log2(1.0 + jnp.abs(block) * (1.0 / CODE_S))), 32767.0)
            code = jnp.where(block < 0.0, -level, level)
            send_out[c, p : p + 4] = code.astype(jnp.int32).astype(jnp.int16)

    def first(c, _):
        @pl.when(c < CHUNKS)
        def _():
            take_rims(0, c)

        step(1, c)
        send_rims(1, c)
        return 0

    def second(c, _):
        take_rims(1, c)
        step(2, c)
        send_rims(2, c)
        return 0

    def third(c, _):
        take_rims(2, c)
        step(3, c)

        @pl.when(c >= 1)
        def _():
            leave(c - 1)

        @pl.when(c >= 2)
        def _():
            swap(send_out, recv_out, out_send_sem, out_recv_sem, c - 1)

        return 0

    def start(c, _):
        arrive(c)
        send_rims(0, c)

        @pl.when(c == 1)
        def _():
            swap(send_in, recv_in, in_send_sem, in_recv_sem, CHUNKS - 1)

        @pl.when(c == 2)
        def _():
            lax.fori_loop(0, 2, first, 0)

        return 0

    lax.fori_loop(0, CHUNKS, start, 0)
    lax.fori_loop(2, 3, first, 0)
    lax.fori_loop(0, 2, second, 0)
    lax.fori_loop(3, CHUNKS + 1, first, 0)
    lax.fori_loop(2, 3, second, 0)
    lax.fori_loop(0, 2, third, 0)
    lax.fori_loop(3, CHUNKS + 1, second, 0)
    swap(send_out, recv_out, out_send_sem, out_recv_sem, 0)
    lax.fori_loop(2, CHUNKS + 1, third, 0)

    def store(c):
        at = pl.ds(c * DEPTH, DEPTH)
        return pltpu.make_async_copy(outv.at[:, at], out_hbm.at[:, at], store_sem.at[c])

    def finish(c, _):
        pltpu.make_async_copy(recv_out.at[c], recv_out.at[c], out_recv_sem.at[c]).wait()
        for side in range(2):
            for gp in range(2):
                code = recv_out[c, side * 16 : side * 16 + 16, gp * 16 : gp * 16 + 16, :]
                level = code.astype(jnp.int32).astype(jnp.float32)
                for e in range(2):
                    block = level[:, e * 8 : e * 8 + 8, :].reshape(128, 128).T.astype(jnp.int32).astype(jnp.int16)
                    outv[2 * gp + e, pl.ds(c * DEPTH, DEPTH), side * ROWS : (side + 1) * ROWS, :] = block.reshape(
                        DEPTH, ROWS, 128
                    )
        store(c).start()
        return 0

    lax.fori_loop(0, CHUNKS, finish, 0)
    for c in range(CHUNKS):
        store(c).wait()
    most = pl.ds(0, PEERS - 1)
    pltpu.make_async_copy(send_in.at[:, most], send_in.at[:, most], in_send_sem).wait()
    pltpu.make_async_copy(send_out.at[:, most], send_out.at[:, most], out_send_sem).wait()
    pltpu.make_async_copy(rim_send, rim_send, rim_send_sem).wait()
    for n, count in ((0, 7), (1, 3)):
        sent = coef_recv.at[0, pl.ds(0, count)]
        pltpu.make_async_copy(sent, sent, coef_send_sem.at[n]).wait()


def per_device(n_gx, n_gy, noise, labels, pair_class, class_gain, stiffness, cross, current):
    hbm = pl.BlockSpec(memory_space=pl.ANY)
    dma = pltpu.SemaphoreType.DMA
    f32, bf16, i16 = jnp.float32, jnp.bfloat16, jnp.int16
    code = pl.pallas_call(
        functools.partial(exchange_kernel, n_gx, n_gy),
        out_shape=jax.ShapeDtypeStruct(noise.shape, i16),
        in_specs=[hbm] * 7,
        out_specs=hbm,
        scratch_shapes=[
            pltpu.VMEM((4, LAYERS, 64, 128), f32),
            pltpu.VMEM((LAYERS, ROWS, 128), jnp.int32),
            pltpu.VMEM((3, LAYERS, ROWS, 128), f32),
            pltpu.VMEM((128, 128), jnp.int32),
            pltpu.SMEM((4,), f32),
            pltpu.SMEM((3, 4), f32),
            pltpu.SMEM((4,), f32),
            pltpu.VMEM((4, LAYERS, 64, 128), i16),
            pltpu.VMEM((CHUNKS, PEERS, 32, 128), i16),
            pltpu.VMEM((CHUNKS, PEERS, 32, 128), i16),
            pltpu.VMEM((CHUNKS, PEERS, 32, 128), i16),
            pltpu.VMEM((CHUNKS, PEERS, 32, 128), i16),
            pltpu.VMEM((PEERS * 32, 128), f32),
            pltpu.VMEM((4, LAYERS * 10, 48, 128), f32),
            pltpu.VMEM((3, LAYERS * COLS, ROWS, 128), f32),
            pltpu.VMEM((RIM_SLOTS, RIM_TOTAL, 128), bf16),
            pltpu.VMEM((RIM_SLOTS, RIM_TOTAL, 128), bf16),
            pltpu.VMEM((2, 8, 8, 128), f32),
            pltpu.VMEM((2, 8, 128), f32),
            pltpu.VMEM((5, 8, 128), f32),
            pltpu.VMEM((128, 128), bf16),
            dma((10,)),
            dma((CHUNKS,)),
            dma,
            dma((CHUNKS,)),
            dma,
            dma((CHUNKS,)),
            dma,
            dma((RIM_SLOTS,)),
            dma((2,)),
            dma((2,)),
        ],
        compiler_params=pltpu.CompilerParams(
            collective_id=0, has_side_effects=True, vmem_limit_bytes=60 * 1024 * 1024
        ),
        name="phase_steps",
    )(noise, labels, pair_class, class_gain, stiffness, cross, current)
    level = code.astype(f32) * (1.0 / CODE_K)
    size = jnp.exp2(jnp.abs(level)) * CODE_S - CODE_S
    return jnp.where(level < 0.0, -size, size)


def solution(mesh):
    placed = (
        P("ga", None, "gx", "gy"),
        P(None, "gx", "gy"),
        P(),
        P(),
        P(None, "ga"),
        P("ga"),
        P(None, None, "gx", "gy"),
    )
    return jax.shard_map(
        functools.partial(per_device, mesh.shape["gx"], mesh.shape["gy"]),
        mesh=mesh,
        in_specs=placed,
        out_specs=P("ga", None, "gx", "gy"),
        check_vma=False,
    )
```

```python
import functools

import jax
import jax.numpy as jnp
from jax import lax
from jax.experimental import pallas as pl
from jax.experimental.pallas import tpu as pltpu
from jax.sharding import PartitionSpec as P

MESH = pl.DeviceIdType.MESH
seed_level = 0.7

PEERS, LAYERS, CHUNKS, DEPTH = 32, 16, 4, 4
ROWS, COLS = 32, 8
NOISE_TOP = 0.15
IN_SCALE = 32767.0 / NOISE_TOP
CODE_S = 2.0**-10
CODE_K = 32767.0 / 23.0
DIRS = ((0, -1), (0, 1), (-1, 0), (1, 0), (-1, -1), (-1, 1), (1, -1), (1, 1))
RIM_ROWS = (128, 128, 32, 32, 16, 16, 16, 16)
RIM_AT = (0, 128, 256, 288, 320, 336, 352, 368)
RIM_TOTAL = 384
RIM_BASE = (0, 4, 9)
RIM_SLOTS = 14


def exchange_kernel(
    n_gx,
    n_gy,
    noise_hbm,
    labels_hbm,
    class_hbm,
    gain_hbm,
    stiff_hbm,
    cross_hbm,
    current_hbm,
    out_hbm,
    noise,
    labels,
    current,
    class_ref,
    gain_ref,
    stiff_ref,
    cross_ref,
    outv,
    send_in,
    recv_in,
    send_out,
    recv_out,
    plane,
    field,
    drift,
    sums,
    rim_send,
    rim_recv,
    coef_recv,
    coef_send,
    coef,
    pair_ref,
    load_sem,
    store_sem,
    in_send_sem,
    in_recv_sem,
    out_send_sem,
    out_recv_sem,
    rim_send_sem,
    rim_recv_sem,
    coef_send_sem,
    coef_recv_sem,
):
    gx, gy, ga = lax.axis_index("gx"), lax.axis_index("gy"), lax.axis_index("ga")
    sx, sy = ga // 16, ga % 16

    def neighbour(dx, dy):
        to_gx, to_gy, to_sx, to_sy = gx, gy, sx, sy
        if dx:
            to_sx = 1 - sx
            to_gx = (gx + sx) % n_gx if dx > 0 else (gx + n_gx - 1 + sx) % n_gx
        if dy > 0:
            to_sy = (sy + 1) % 16
            to_gy = (gy + (sy + 1) // 16) % n_gy
        if dy < 0:
            to_sy = (sy + 15) % 16
            to_gy = (gy + n_gy - 1 + (sy + 15) // 16) % n_gy
        return to_gx, to_gy, to_sx * 16 + to_sy

    def peer(k):
        return (gx, gy, (ga + k) % PEERS)

    def noise_load(c):
        at = pl.ds(c * DEPTH, DEPTH)
        return pltpu.make_async_copy(noise_hbm.at[:, at], noise.at[:, at], load_sem.at[c])

    half = pl.ds(pl.multiple_of(sx * ROWS, ROWS), ROWS)
    labels_load = pltpu.make_async_copy(labels_hbm.at[:, half], labels, load_sem.at[4])
    current_load = pltpu.make_async_copy(current_hbm.at[:, :, half], current, load_sem.at[5])
    small = ((stiff_hbm, stiff_ref), (cross_hbm, cross_ref), (gain_hbm, gain_ref), (class_hbm, class_ref))
    small_loads = [pltpu.make_async_copy(a, b, load_sem.at[6 + n]) for n, (a, b) in enumerate(small)]
    noise_load(0).start()
    for load in small_loads:
        load.start()
    for c in range(1, CHUNKS):
        noise_load(c).start()
    labels_load.start()
    current_load.start()

    barrier = pltpu.get_barrier_semaphore()

    def greet(k, _):
        pl.semaphore_signal(barrier, inc=1, device_id=peer(k), device_id_type=MESH)
        return 0

    lax.fori_loop(1, PEERS, greet, 0)
    for dx, dy in DIRS:
        pl.semaphore_signal(barrier, inc=1, device_id=neighbour(dx, dy), device_id_type=MESH)

    small_loads[0].wait()
    small_loads[1].wait()
    lane = lax.broadcasted_iota(jnp.int32, (1, 128), 1)
    rows = []
    for r in range(4):
        row = jnp.zeros((1, 128), jnp.float32)
        for k in range(4):
            value = stiff_ref[r, k] if r < 3 else cross_ref[k]
            row = jnp.where(lane == ga * 4 + k, value, row)
        rows.append(row)
    coef_send[0] = jnp.concatenate(rows + [jnp.zeros((4, 128), jnp.float32)], axis=0)

    def encode_in(c):
        for side in range(2):
            for gp in range(2):
                parts = []
                for g in (2 * gp, 2 * gp + 1):
                    block = noise[g, pl.ds(c * DEPTH, DEPTH), side * ROWS : (side + 1) * ROWS, :]
                    code = jnp.round(block.reshape(128, 128).T * IN_SCALE)
                    parts.append(code.reshape(16, 8, 128))
                both = jnp.concatenate(parts, axis=1).astype(jnp.int32).astype(jnp.int16)
                send_in[c, side * 16 : side * 16 + 16, gp * 16 : gp * 16 + 16, :] = both

    noise_load(0).wait()
    encode_in(0)
    pl.semaphore_wait(barrier, PEERS - 1 + len(DIRS))

    chip = sy // 2

    def coef_first(k):
        to = sx * 16 + ((chip + k) % 8) * 2 + sy % 2
        return pltpu.make_async_remote_copy(
            coef_send.at[0], coef_recv.at[0, chip], coef_send_sem.at[0], coef_recv_sem.at[0],
            device_id=(gx, gy, to), device_id_type=MESH,
        )

    group = sx * 2 + sy % 2

    def coef_second(k):
        to = (group + k) % 4
        return pltpu.make_async_remote_copy(
            coef_send.at[1], coef_recv.at[1, group], coef_send_sem.at[1], coef_recv_sem.at[1],
            device_id=(gx, gy, (to // 2) * 16 + chip * 2 + to % 2), device_id_type=MESH,
        )

    for k in range(1, 8):
        coef_first(k).start()
    pltpu.make_async_copy(coef_send.at[0], coef_recv.at[0, chip], coef_recv_sem.at[0]).start()

    def swap(send, recv, send_sem, recv_sem, c):
        def one(k, _):
            to = (ga + k) % PEERS
            pltpu.make_async_remote_copy(
                send.at[c, to], recv.at[c, ga], send_sem, recv_sem.at[c],
                device_id=(gx, gy, to), device_id_type=MESH,
            ).start()
            return 0

        lax.fori_loop(1, PEERS, one, 0)
        pltpu.make_async_copy(send.at[c, ga], recv.at[c, ga], recv_sem.at[c]).start()

    swap(send_in, recv_in, in_send_sem, in_recv_sem, 0)
    for c in range(1, CHUNKS):
        noise_load(c).wait()
        encode_in(c)
        if c < CHUNKS - 1:
            swap(send_in, recv_in, in_send_sem, in_recv_sem, c)

    small_loads[2].wait()
    small_loads[3].wait()
    picked = jnp.zeros((128, 128), jnp.float32)
    for k in range(4):
        picked = jnp.where(class_ref[...] == k, gain_ref[k], picked)
    row_id = lax.broadcasted_iota(jnp.int32, (128, 128), 0)
    col_id = lax.broadcasted_iota(jnp.int32, (128, 128), 1)
    symmetric = jnp.where(row_id == col_id, 0.0, 0.5 * (picked + picked.T))
    pair_ref[...] = (symmetric.astype(jnp.bfloat16).astype(jnp.float32) * 2.0).astype(jnp.bfloat16)

    labels_load.wait()
    current_load.wait()
    shift = (128 - sy * COLS) % 128
    grain = lax.broadcasted_iota(jnp.int32, (ROWS, 128), 1)

    def spread(z, _):
        own = pltpu.roll(labels[z], shift, 1)
        for y in range(COLS):
            column = jnp.broadcast_to(own[:, y : y + 1], (ROWS, 128))
            field[0, z * 10 + y + 1, 8:40, :] = jnp.where(column == grain, seed_level, 0.0)
        for k in range(3):
            flow = pltpu.roll(current[k, z] * 0.05, shift, 1)
            for y in range(COLS):
                drift[k, z * COLS + y] = jnp.broadcast_to(flow[:, y : y + 1], (ROWS, 128))
        return 0

    pltpu.make_async_copy(coef_recv.at[0], coef_recv.at[0], coef_recv_sem.at[0]).wait()
    coef_send[1] = jnp.sum(coef_recv[0], axis=0)
    for k in range(1, 4):
        coef_second(k).start()
    pltpu.make_async_copy(coef_send.at[1], coef_recv.at[1, group], coef_recv_sem.at[1]).start()

    lax.fori_loop(0, LAYERS, spread, 0)

    quarter = coef_recv.at[1, pl.ds(0, 4)]
    pltpu.make_async_copy(quarter, quarter, coef_recv_sem.at[1]).wait()
    total = jnp.sum(coef_recv[1, 0:4], axis=0)
    k_x, k_y, k_z, k_xy = (jnp.broadcast_to(total[r : r + 1], (8, 128)) for r in range(4))
    coef[0] = 1.1 - 0.2 * (k_x + k_y + k_z)
    coef[1] = 0.1 * k_x
    coef[2] = 0.1 * k_y
    coef[3] = 0.1 * k_z
    coef[4] = 0.05 * k_xy

    def arrive(c):
        pltpu.make_async_copy(recv_in.at[c], recv_in.at[c], in_recv_sem.at[c]).wait()
        for p in range(0, PEERS, 4):
            block = recv_in[c, p : p + 4].astype(jnp.int32).astype(jnp.float32) * (1.0 / IN_SCALE)
            plane[p * 32 : (p + 4) * 32, :] = block.reshape(128, 128)
        for y in range(COLS):
            block = plane[pl.ds(y, 128, stride=8), :].T
            for d in range(DEPTH):
                at = (c * DEPTH + d) * 10 + y + 1
                field[0, at, 8:40, :] = field[0, at, 8:40, :] + block[d * ROWS : (d + 1) * ROWS]

    def layer_of(c, s, d):
        return jnp.clip(c * DEPTH - s + d, 0, LAYERS - 1)

    def rim_copies(s, c):
        slot = RIM_BASE[s] + c
        for n in (4, 5, 6, 7, 2, 3, 0, 1):
            dx, dy = DIRS[n]
            m = DIRS.index((-dx, -dy))
            yield pltpu.make_async_remote_copy(
                rim_send.at[slot, pl.ds(RIM_AT[n], RIM_ROWS[n])], rim_recv.at[slot, pl.ds(RIM_AT[m], RIM_ROWS[m])],
                rim_send_sem, rim_recv_sem.at[slot], device_id=neighbour(dx, dy), device_id_type=MESH,
            )

    flat = field.reshape(4, LAYERS * 10 * 48, 128)

    def send_rims(s, c):
        slot = RIM_BASE[s] + c
        layers = [layer_of(c, s, d) for d in range(DEPTH)]
        for d, z in enumerate(layers):
            rim_send[slot, d * ROWS : (d + 1) * ROWS, :] = field[s, z * 10 + 1, 8:40, :].astype(jnp.bfloat16)
            rim_send[slot, 128 + d * ROWS : 128 + (d + 1) * ROWS, :] = field[s, z * 10 + 8, 8:40, :].astype(jnp.bfloat16)
        for n, x in ((2, 8), (3, 39)):
            for d in range(0, DEPTH, 2):
                pieces = [flat[s, pl.ds((layers[e] * 10 + 1) * 48 + x, COLS, stride=48), :] for e in (d, d + 1)]
                at = RIM_AT[n] + d * COLS
                rim_send[slot, at : at + 16, :] = jnp.concatenate(pieces, axis=0).astype(jnp.bfloat16)
        for n, (y, x) in ((4, (1, 8)), (5, (8, 8)), (6, (1, 39)), (7, (8, 39))):
            pieces = [field[s, z * 10 + y, x : x + 1, :] for z in layers] + [jnp.zeros((12, 128), jnp.float32)]
            rim_send[slot, RIM_AT[n] : RIM_AT[n] + 16, :] = jnp.concatenate(pieces, axis=0).astype(jnp.bfloat16)
        for copy in rim_copies(s, c):
            copy.start()

    def take_rims(s, c):
        slot = RIM_BASE[s] + c
        pltpu.make_async_copy(rim_recv.at[slot], rim_recv.at[slot], rim_recv_sem.at[slot]).wait()
        layers = [layer_of(c, s, d) for d in range(DEPTH)]
        for d, z in enumerate(layers):
            field[s, z * 10, 8:40, :] = rim_recv[slot, d * ROWS : (d + 1) * ROWS, :].astype(jnp.float32)
            field[s, z * 10 + 9, 8:40, :] = rim_recv[slot, 128 + d * ROWS : 128 + (d + 1) * ROWS, :].astype(jnp.float32)
        for n, x in ((2, 7), (3, 40)):
            for d in range(0, DEPTH, 2):
                at = RIM_AT[n] + d * COLS
                pieces = rim_recv[slot, at : at + 16, :].astype(jnp.float32)
                for e in (0, 1):
                    flat[s, pl.ds((layers[d + e] * 10 + 1) * 48 + x, COLS, stride=48), :] = pieces[e * 8 : e * 8 + 8]
        for n, (y, x) in ((4, (0, 7)), (5, (9, 7)), (6, (0, 40)), (7, (9, 40))):
            pieces = rim_recv[slot, RIM_AT[n] : RIM_AT[n] + 16, :].astype(jnp.float32)
            for d, z in enumerate(layers):
                field[s, z * 10 + y, x : x + 1, :] = pieces[d : d + 1]

    def couple(s, c):
        for d in range(DEPTH):
            z = layer_of(c, s, d)
            squares = [jnp.square(field[s - 1, z * 10 + y + 1, 8:40, :]).astype(jnp.bfloat16) for y in range(COLS)]
            sums[d] = jnp.dot(jnp.concatenate(squares, axis=0), pair_ref[...], preferred_element_type=jnp.float32)

    def step(s, c):
        def one(z, _):
            here = z * 10
            above = jnp.minimum(z + 1, LAYERS - 1) * 10
            below = jnp.maximum(z - 1, 0) * 10
            from_base = z - (c * DEPTH - s)

            def wide(n):
                return jnp.concatenate([coef[n]] * 4, axis=0)

            a_0, a_x, a_y, a_z, a_xy = (wide(n) for n in range(5))

            def slope(y):
                return field[s - 1, here + y + 1, 9:41, :] - field[s - 1, here + y + 1, 7:39, :]

            slopes = [slope(-1), slope(0)]
            for y in range(COLS):
                slopes.append(slope(y + 1))
                v = field[s - 1, here + y + 1, 8:40, :]
                x_p, x_m = field[s - 1, here + y + 1, 9:41, :], field[s - 1, here + y + 1, 7:39, :]
                y_p, y_m = field[s - 1, here + y + 2, 8:40, :], field[s - 1, here + y, 8:40, :]
                z_p, z_m = field[s - 1, above + y + 1, 8:40, :], field[s - 1, below + y + 1, 8:40, :]
                new = v * (a_0 - 0.1 * (v * v + sums[from_base, y * ROWS : (y + 1) * ROWS, :]))
                new = new + a_x * (x_p + x_m) + a_y * (y_p + y_m) + a_z * (z_p + z_m)
                new = new + a_xy * (slopes[y + 2] - slopes[y])
                at = z * COLS + y
                new = new - (drift[0, at] * slopes[y + 1] + drift[1, at] * (y_p - y_m) + drift[2, at] * (z_p - z_m))
                field[s, here + y + 1, 8:40, :] = new
            return 0

        first = jnp.maximum(c * DEPTH - s, 0)
        last = jnp.minimum(c * DEPTH - s + DEPTH, LAYERS)
        lax.fori_loop(first, last, one, 0)

    def leave(c):
        for y in range(COLS):
            parts = [field[3, (c * DEPTH + d) * 10 + y + 1, 8:40, :] for d in range(DEPTH)]
            plane[pl.ds(y, 128, stride=8), :] = jnp.concatenate(parts, axis=0).T
        for p in range(0, PEERS, 4):
            block = plane[p * 32 : (p + 4) * 32, :].reshape(4, 32, 128)
            level = jnp.minimum(jnp.round(CODE_K * jnp.log2(1.0 + jnp.abs(block) * (1.0 / CODE_S))), 32767.0)
            code = jnp.where(block < 0.0, -level, level)
            send_out[c, p : p + 4] = code.astype(jnp.int32).astype(jnp.int16)

    def first(c, _):
        couple(1, c)

        @pl.when(c < CHUNKS)
        def _():
            take_rims(0, c)

        step(1, c)
        send_rims(1, c)
        return 0

    def second(c, _):
        couple(2, c)
        take_rims(1, c)
        step(2, c)
        send_rims(2, c)
        return 0

    def third(c, _):
        couple(3, c)
        take_rims(2, c)
        step(3, c)

        @pl.when(c >= 1)
        def _():
            leave(c - 1)

        @pl.when(c >= 2)
        def _():
            swap(send_out, recv_out, out_send_sem, out_recv_sem, c - 1)

        return 0

    def start(c, _):
        arrive(c)
        send_rims(0, c)

        @pl.when(c == 1)
        def _():
            swap(send_in, recv_in, in_send_sem, in_recv_sem, CHUNKS - 1)

        @pl.when(c == 2)
        def _():
            lax.fori_loop(0, 2, first, 0)

        return 0

    lax.fori_loop(0, CHUNKS, start, 0)
    lax.fori_loop(2, 3, first, 0)
    lax.fori_loop(0, 2, second, 0)
    lax.fori_loop(3, CHUNKS + 1, first, 0)
    lax.fori_loop(2, 3, second, 0)
    lax.fori_loop(0, 2, third, 0)
    lax.fori_loop(3, CHUNKS + 1, second, 0)
    swap(send_out, recv_out, out_send_sem, out_recv_sem, 0)
    lax.fori_loop(2, CHUNKS + 1, third, 0)

    def store(c):
        at = pl.ds(c * DEPTH, DEPTH)
        return pltpu.make_async_copy(outv.at[:, at], out_hbm.at[:, at], store_sem.at[c])

    def finish(c, _):
        pltpu.make_async_copy(recv_out.at[c], recv_out.at[c], out_recv_sem.at[c]).wait()
        for side in range(2):
            for gp in range(2):
                code = recv_out[c, side * 16 : side * 16 + 16, gp * 16 : gp * 16 + 16, :]
                level = code.astype(jnp.int32).astype(jnp.float32)
                for e in range(2):
                    block = level[:, e * 8 : e * 8 + 8, :].reshape(128, 128).T.astype(jnp.int32).astype(jnp.int16)
                    outv[2 * gp + e, pl.ds(c * DEPTH, DEPTH), side * ROWS : (side + 1) * ROWS, :] = block.reshape(
                        DEPTH, ROWS, 128
                    )
        store(c).start()
        return 0

    lax.fori_loop(0, CHUNKS, finish, 0)
    for c in range(CHUNKS):
        store(c).wait()
    most = pl.ds(0, PEERS - 1)
    pltpu.make_async_copy(send_in.at[:, most], send_in.at[:, most], in_send_sem).wait()
    pltpu.make_async_copy(send_out.at[:, most], send_out.at[:, most], out_send_sem).wait()
    pltpu.make_async_copy(rim_send, rim_send, rim_send_sem).wait()
    for n, count in ((0, 7), (1, 3)):
        sent = coef_recv.at[0, pl.ds(0, count)]
        pltpu.make_async_copy(sent, sent, coef_send_sem.at[n]).wait()


def per_device(n_gx, n_gy, noise, labels, pair_class, class_gain, stiffness, cross, current):
    hbm = pl.BlockSpec(memory_space=pl.ANY)
    dma = pltpu.SemaphoreType.DMA
    f32, bf16, i16 = jnp.float32, jnp.bfloat16, jnp.int16
    code = pl.pallas_call(
        functools.partial(exchange_kernel, n_gx, n_gy),
        out_shape=jax.ShapeDtypeStruct(noise.shape, i16),
        in_specs=[hbm] * 7,
        out_specs=hbm,
        scratch_shapes=[
            pltpu.VMEM((4, LAYERS, 64, 128), f32),
            pltpu.VMEM((LAYERS, ROWS, 128), jnp.int32),
            pltpu.VMEM((3, LAYERS, ROWS, 128), f32),
            pltpu.VMEM((128, 128), jnp.int32),
            pltpu.SMEM((4,), f32),
            pltpu.SMEM((3, 4), f32),
            pltpu.SMEM((4,), f32),
            pltpu.VMEM((4, LAYERS, 64, 128), i16),
            pltpu.VMEM((CHUNKS, PEERS, 32, 128), i16),
            pltpu.VMEM((CHUNKS, PEERS, 32, 128), i16),
            pltpu.VMEM((CHUNKS, PEERS, 32, 128), i16),
            pltpu.VMEM((CHUNKS, PEERS, 32, 128), i16),
            pltpu.VMEM((PEERS * 32, 128), f32),
            pltpu.VMEM((4, LAYERS * 10, 48, 128), f32),
            pltpu.VMEM((3, LAYERS * COLS, ROWS, 128), f32),
            pltpu.VMEM((DEPTH, COLS * ROWS, 128), f32),
            pltpu.VMEM((RIM_SLOTS, RIM_TOTAL, 128), bf16),
            pltpu.VMEM((RIM_SLOTS, RIM_TOTAL, 128), bf16),
            pltpu.VMEM((2, 8, 8, 128), f32),
            pltpu.VMEM((2, 8, 128), f32),
            pltpu.VMEM((5, 8, 128), f32),
            pltpu.VMEM((128, 128), bf16),
            dma((10,)),
            dma((CHUNKS,)),
            dma,
            dma((CHUNKS,)),
            dma,
            dma((CHUNKS,)),
            dma,
            dma((RIM_SLOTS,)),
            dma((2,)),
            dma((2,)),
        ],
        compiler_params=pltpu.CompilerParams(
            collective_id=0, has_side_effects=True, vmem_limit_bytes=60 * 1024 * 1024
        ),
        name="phase_steps",
    )(noise, labels, pair_class, class_gain, stiffness, cross, current)
    level = code.astype(f32) * (1.0 / CODE_K)
    size = jnp.exp2(jnp.abs(level)) * CODE_S - CODE_S
    return jnp.where(level < 0.0, -size, size)


def solution(mesh):
    placed = (
        P("ga", None, "gx", "gy"),
        P(None, "gx", "gy"),
        P(),
        P(),
        P(None, "ga"),
        P("ga"),
        P(None, None, "gx", "gy"),
    )
    return jax.shard_map(
        functools.partial(per_device, mesh.shape["gx"], mesh.shape["gy"]),
        mesh=mesh,
        in_specs=placed,
        out_specs=P("ga", None, "gx", "gy"),
        check_vma=False,
    )
```

```python
import functools

import jax
import jax.numpy as jnp
from jax import lax
from jax.experimental import pallas as pl
from jax.experimental.pallas import tpu as pltpu
from jax.sharding import PartitionSpec as P

MESH = pl.DeviceIdType.MESH
seed_level = 0.7

PEERS, LAYERS, CHUNKS, DEPTH = 32, 16, 4, 4
ROWS, COLS = 32, 8
NOISE_TOP = 0.15
IN_SCALE = 32767.0 / NOISE_TOP
CODE_S = 2.0**-10
CODE_K = 32767.0 / 23.0
DIRS = ((0, -1), (0, 1), (-1, 0), (1, 0), (-1, -1), (-1, 1), (1, -1), (1, 1))
RIM_ROWS = (128, 128, 32, 32, 16, 16, 16, 16)
RIM_AT = (0, 128, 256, 288, 320, 336, 352, 368)
RIM_TOTAL = 384
RIM_BASE = (0, 4, 9)
RIM_SLOTS = 14
HALF = 8


def exchange_kernel(
    n_gx,
    n_gy,
    noise_hbm,
    labels_hbm,
    class_hbm,
    gain_hbm,
    stiff_hbm,
    cross_hbm,
    current_hbm,
    out_hbm,
    noise,
    labels,
    current,
    class_ref,
    gain_ref,
    stiff_ref,
    cross_ref,
    outv,
    send_in,
    recv_in,
    send_out,
    recv_out,
    plane,
    field,
    drift,
    sums,
    rim_send,
    rim_recv,
    coef_recv,
    coef_send,
    coef,
    pair_ref,
    load_sem,
    store_sem,
    in_send_sem,
    in_recv_sem,
    out_send_sem,
    out_recv_sem,
    rim_send_sem,
    rim_recv_sem,
    coef_send_sem,
    coef_recv_sem,
):
    gx, gy, ga = lax.axis_index("gx"), lax.axis_index("gy"), lax.axis_index("ga")
    sx, sy = ga // 16, ga % 16

    def neighbour(dx, dy):
        to_gx, to_gy, to_sx, to_sy = gx, gy, sx, sy
        if dx:
            to_sx = 1 - sx
            to_gx = (gx + sx) % n_gx if dx > 0 else (gx + n_gx - 1 + sx) % n_gx
        if dy > 0:
            to_sy = (sy + 1) % 16
            to_gy = (gy + (sy + 1) // 16) % n_gy
        if dy < 0:
            to_sy = (sy + 15) % 16
            to_gy = (gy + n_gy - 1 + (sy + 15) // 16) % n_gy
        return to_gx, to_gy, to_sx * 16 + to_sy

    def peer(k):
        return (gx, gy, (ga + k) % PEERS)

    def noise_load(c):
        at = pl.ds(c * DEPTH, DEPTH)
        return pltpu.make_async_copy(noise_hbm.at[:, at], noise.at[:, at], load_sem.at[c])

    half = pl.ds(pl.multiple_of(sx * ROWS, ROWS), ROWS)
    labels_load = pltpu.make_async_copy(labels_hbm.at[:, half], labels, load_sem.at[4])
    current_load = pltpu.make_async_copy(current_hbm.at[:, :, half], current, load_sem.at[5])
    small = ((stiff_hbm, stiff_ref), (cross_hbm, cross_ref), (gain_hbm, gain_ref), (class_hbm, class_ref))
    small_loads = [pltpu.make_async_copy(a, b, load_sem.at[6 + n]) for n, (a, b) in enumerate(small)]
    noise_load(0).start()
    for load in small_loads:
        load.start()
    for c in range(1, CHUNKS):
        noise_load(c).start()
    labels_load.start()
    current_load.start()

    barrier = pltpu.get_barrier_semaphore()

    def greet(k, _):
        pl.semaphore_signal(barrier, inc=1, device_id=peer(k), device_id_type=MESH)
        return 0

    lax.fori_loop(1, PEERS, greet, 0)
    for dx, dy in DIRS:
        pl.semaphore_signal(barrier, inc=1, device_id=neighbour(dx, dy), device_id_type=MESH)

    small_loads[0].wait()
    small_loads[1].wait()
    lane = lax.broadcasted_iota(jnp.int32, (1, 128), 1)
    rows = []
    for r in range(4):
        row = jnp.zeros((1, 128), jnp.float32)
        for k in range(4):
            value = stiff_ref[r, k] if r < 3 else cross_ref[k]
            row = jnp.where(lane == ga * 4 + k, value, row)
        rows.append(row)
    coef_send[0] = jnp.concatenate(rows + [jnp.zeros((4, 128), jnp.float32)], axis=0)

    def encode_in(c):
        for side in range(2):
            for gp in range(2):
                parts = []
                for g in (2 * gp, 2 * gp + 1):
                    block = noise[g, pl.ds(c * DEPTH, DEPTH), side * ROWS : (side + 1) * ROWS, :]
                    code = jnp.round(block.reshape(128, 128).T * IN_SCALE)
                    parts.append(code.reshape(16, 8, 128))
                both = jnp.concatenate(parts, axis=1).astype(jnp.int32).astype(jnp.int16)
                send_in[c, side * 16 : side * 16 + 16, gp * 16 : gp * 16 + 16, :] = both

    noise_load(0).wait()
    encode_in(0)
    pl.semaphore_wait(barrier, PEERS - 1 + len(DIRS))

    chip = sy // 2

    def coef_first(k):
        to = sx * 16 + ((chip + k) % 8) * 2 + sy % 2
        return pltpu.make_async_remote_copy(
            coef_send.at[0], coef_recv.at[0, chip], coef_send_sem.at[0], coef_recv_sem.at[0],
            device_id=(gx, gy, to), device_id_type=MESH,
        )

    group = sx * 2 + sy % 2

    def coef_second(k):
        to = (group + k) % 4
        return pltpu.make_async_remote_copy(
            coef_send.at[1], coef_recv.at[1, group], coef_send_sem.at[1], coef_recv_sem.at[1],
            device_id=(gx, gy, (to // 2) * 16 + chip * 2 + to % 2), device_id_type=MESH,
        )

    for k in range(1, 8):
        coef_first(k).start()
    pltpu.make_async_copy(coef_send.at[0], coef_recv.at[0, chip], coef_recv_sem.at[0]).start()

    def swap(send, recv, send_sem, recv_sem, c, low=1, high=PEERS):
        def one(k, _):
            to = (ga + k) % PEERS
            pltpu.make_async_remote_copy(
                send.at[c, to], recv.at[c, ga], send_sem, recv_sem.at[c],
                device_id=(gx, gy, to), device_id_type=MESH,
            ).start()
            return 0

        lax.fori_loop(low, high, one, 0)
        if low == 1:
            pltpu.make_async_copy(send.at[c, ga], recv.at[c, ga], recv_sem.at[c]).start()

    swap(send_in, recv_in, in_send_sem, in_recv_sem, 0)
    for c in range(1, CHUNKS):
        noise_load(c).wait()
        encode_in(c)
        if c < CHUNKS - 1:
            swap(send_in, recv_in, in_send_sem, in_recv_sem, c)

    small_loads[2].wait()
    small_loads[3].wait()
    picked = jnp.zeros((128, 128), jnp.float32)
    for k in range(4):
        picked = jnp.where(class_ref[...] == k, gain_ref[k], picked)
    row_id = lax.broadcasted_iota(jnp.int32, (128, 128), 0)
    col_id = lax.broadcasted_iota(jnp.int32, (128, 128), 1)
    symmetric = jnp.where(row_id == col_id, 0.0, 0.5 * (picked + picked.T))
    pair_ref[...] = (symmetric.astype(jnp.bfloat16).astype(jnp.float32) * 2.0).astype(jnp.bfloat16)

    labels_load.wait()
    current_load.wait()
    shift = (128 - sy * COLS) % 128
    grain = lax.broadcasted_iota(jnp.int32, (ROWS, 128), 1)

    def spread(z, _):
        own = pltpu.roll(labels[z], shift, 1)
        for y in range(COLS):
            column = jnp.broadcast_to(own[:, y : y + 1], (ROWS, 128))
            field[0, z * 10 + y + 1, 8:40, :] = jnp.where(column == grain, seed_level, 0.0)
        for k in range(3):
            flow = pltpu.roll(current[k, z] * 0.05, shift, 1)
            for y in range(COLS):
                drift[k, z * COLS + y] = jnp.broadcast_to(flow[:, y : y + 1], (ROWS, 128))
        return 0

    pltpu.make_async_copy(coef_recv.at[0], coef_recv.at[0], coef_recv_sem.at[0]).wait()
    coef_send[1] = jnp.sum(coef_recv[0], axis=0)
    for k in range(1, 4):
        coef_second(k).start()
    pltpu.make_async_copy(coef_send.at[1], coef_recv.at[1, group], coef_recv_sem.at[1]).start()

    lax.fori_loop(0, LAYERS, spread, 0)

    quarter = coef_recv.at[1, pl.ds(0, 4)]
    pltpu.make_async_copy(quarter, quarter, coef_recv_sem.at[1]).wait()
    total = jnp.sum(coef_recv[1, 0:4], axis=0)
    k_x, k_y, k_z, k_xy = (jnp.broadcast_to(total[r : r + 1], (8, 128)) for r in range(4))
    coef[0] = 1.1 - 0.2 * (k_x + k_y + k_z)
    coef[1] = 0.1 * k_x
    coef[2] = 0.1 * k_y
    coef[3] = 0.1 * k_z
    coef[4] = 0.05 * k_xy

    def arrive(c):
        pltpu.make_async_copy(recv_in.at[c], recv_in.at[c], in_recv_sem.at[c]).wait()
        for p in range(0, PEERS, 4):
            block = recv_in[c, p : p + 4].astype(jnp.int32).astype(jnp.float32) * (1.0 / IN_SCALE)
            plane[p * 32 : (p + 4) * 32, :] = block.reshape(128, 128)
        for y in range(COLS):
            block = plane[pl.ds(y, 128, stride=8), :].T
            for d in range(DEPTH):
                at = (c * DEPTH + d) * 10 + y + 1
                field[0, at, 8:40, :] = field[0, at, 8:40, :] + block[d * ROWS : (d + 1) * ROWS]

    def layer_of(c, s, d):
        return jnp.clip(c * DEPTH - s + d, 0, LAYERS - 1)

    def rim_copies(s, c):
        slot = RIM_BASE[s] + c
        for n in (4, 5, 6, 7, 2, 3, 0, 1):
            dx, dy = DIRS[n]
            m = DIRS.index((-dx, -dy))
            yield pltpu.make_async_remote_copy(
                rim_send.at[slot, pl.ds(RIM_AT[n], RIM_ROWS[n])], rim_recv.at[slot, pl.ds(RIM_AT[m], RIM_ROWS[m])],
                rim_send_sem, rim_recv_sem.at[slot], device_id=neighbour(dx, dy), device_id_type=MESH,
            )

    flat = field.reshape(4, LAYERS * 10 * 48, 128)

    def send_rims(s, c):
        slot = RIM_BASE[s] + c
        layers = [layer_of(c, s, d) for d in range(DEPTH)]
        for d, z in enumerate(layers):
            rim_send[slot, d * ROWS : (d + 1) * ROWS, :] = field[s, z * 10 + 1, 8:40, :].astype(jnp.bfloat16)
            rim_send[slot, 128 + d * ROWS : 128 + (d + 1) * ROWS, :] = field[s, z * 10 + 8, 8:40, :].astype(jnp.bfloat16)
        for n, x in ((2, 8), (3, 39)):
            for d in range(0, DEPTH, 2):
                pieces = [flat[s, pl.ds((layers[e] * 10 + 1) * 48 + x, COLS, stride=48), :] for e in (d, d + 1)]
                at = RIM_AT[n] + d * COLS
                rim_send[slot, at : at + 16, :] = jnp.concatenate(pieces, axis=0).astype(jnp.bfloat16)
        for n, (y, x) in ((4, (1, 8)), (5, (8, 8)), (6, (1, 39)), (7, (8, 39))):
            pieces = [field[s, z * 10 + y, x : x + 1, :] for z in layers] + [jnp.zeros((12, 128), jnp.float32)]
            rim_send[slot, RIM_AT[n] : RIM_AT[n] + 16, :] = jnp.concatenate(pieces, axis=0).astype(jnp.bfloat16)
        for copy in rim_copies(s, c):
            copy.start()

    def take_rims(s, c):
        slot = RIM_BASE[s] + c
        pltpu.make_async_copy(rim_recv.at[slot], rim_recv.at[slot], rim_recv_sem.at[slot]).wait()
        layers = [layer_of(c, s, d) for d in range(DEPTH)]
        for d, z in enumerate(layers):
            field[s, z * 10, 8:40, :] = rim_recv[slot, d * ROWS : (d + 1) * ROWS, :].astype(jnp.float32)
            field[s, z * 10 + 9, 8:40, :] = rim_recv[slot, 128 + d * ROWS : 128 + (d + 1) * ROWS, :].astype(jnp.float32)
        for n, x in ((2, 7), (3, 40)):
            for d in range(0, DEPTH, 2):
                at = RIM_AT[n] + d * COLS
                pieces = rim_recv[slot, at : at + 16, :].astype(jnp.float32)
                for e in (0, 1):
                    flat[s, pl.ds((layers[d + e] * 10 + 1) * 48 + x, COLS, stride=48), :] = pieces[e * 8 : e * 8 + 8]
        for n, (y, x) in ((4, (0, 7)), (5, (9, 7)), (6, (0, 40)), (7, (9, 40))):
            pieces = rim_recv[slot, RIM_AT[n] : RIM_AT[n] + 16, :].astype(jnp.float32)
            for d, z in enumerate(layers):
                field[s, z * 10 + y, x : x + 1, :] = pieces[d : d + 1]

    def couple(s, c):
        for d in range(DEPTH):
            z = layer_of(c, s, d)
            squares = [jnp.square(field[s - 1, z * 10 + y + 1, 8:40, :]).astype(jnp.bfloat16) for y in range(COLS)]
            sums[d] = jnp.dot(jnp.concatenate(squares, axis=0), pair_ref[...], preferred_element_type=jnp.float32)

    def step(s, c):
        def one(z, _):
            here = z * 10
            above = jnp.minimum(z + 1, LAYERS - 1) * 10
            below = jnp.maximum(z - 1, 0) * 10
            from_base = z - (c * DEPTH - s)

            def wide(n):
                return jnp.concatenate([coef[n]] * 4, axis=0)

            a_0, a_x, a_y, a_z, a_xy = (wide(n) for n in range(5))

            def slope(y):
                return field[s - 1, here + y + 1, 9:41, :] - field[s - 1, here + y + 1, 7:39, :]

            slopes = [slope(-1), slope(0)]
            for y in range(COLS):
                slopes.append(slope(y + 1))
                v = field[s - 1, here + y + 1, 8:40, :]
                x_p, x_m = field[s - 1, here + y + 1, 9:41, :], field[s - 1, here + y + 1, 7:39, :]
                y_p, y_m = field[s - 1, here + y + 2, 8:40, :], field[s - 1, here + y, 8:40, :]
                z_p, z_m = field[s - 1, above + y + 1, 8:40, :], field[s - 1, below + y + 1, 8:40, :]
                new = v * (a_0 - 0.1 * (v * v + sums[from_base, y * ROWS : (y + 1) * ROWS, :]))
                new = new + a_x * (x_p + x_m) + a_y * (y_p + y_m) + a_z * (z_p + z_m)
                new = new + a_xy * (slopes[y + 2] - slopes[y])
                at = z * COLS + y
                new = new - (drift[0, at] * slopes[y + 1] + drift[1, at] * (y_p - y_m) + drift[2, at] * (z_p - z_m))
                field[s, here + y + 1, 8:40, :] = new
            return 0

        first = jnp.maximum(c * DEPTH - s, 0)
        last = jnp.minimum(c * DEPTH - s + DEPTH, LAYERS)
        lax.fori_loop(first, last, one, 0)

    def leave(c):
        for y in range(COLS):
            parts = [field[3, (c * DEPTH + d) * 10 + y + 1, 8:40, :] for d in range(DEPTH)]
            plane[pl.ds(y, 128, stride=8), :] = jnp.concatenate(parts, axis=0).T
        for p in range(0, PEERS, 4):
            block = plane[p * 32 : (p + 4) * 32, :].reshape(4, 32, 128)
            level = jnp.minimum(jnp.round(CODE_K * jnp.log2(1.0 + jnp.abs(block) * (1.0 / CODE_S))), 32767.0)
            code = jnp.where(block < 0.0, -level, level)
            send_out[c, p : p + 4] = code.astype(jnp.int32).astype(jnp.int16)

    def first(c, _):
        couple(1, c)

        @pl.when(c < CHUNKS)
        def _():
            take_rims(0, c)

        step(1, c)
        send_rims(1, c)
        return 0

    def second(c, _):
        couple(2, c)
        take_rims(1, c)
        step(2, c)
        send_rims(2, c)
        return 0

    def third(c, _):
        couple(3, c)
        take_rims(2, c)
        step(3, c)

        @pl.when(c >= 1)
        def _():
            leave(c - 1)

        @pl.when(c >= 2)
        def _():
            swap(send_out, recv_out, out_send_sem, out_recv_sem, c - 1)

        return 0

    def start(c, _):
        arrive(c)
        send_rims(0, c)

        @pl.when(c == 1)
        def _():
            swap(send_in, recv_in, in_send_sem, in_recv_sem, CHUNKS - 1)

        @pl.when(c == 2)
        def _():
            lax.fori_loop(0, 2, first, 0)

        return 0

    lax.fori_loop(0, CHUNKS, start, 0)
    lax.fori_loop(2, 3, first, 0)
    lax.fori_loop(0, 2, second, 0)
    lax.fori_loop(3, CHUNKS + 1, first, 0)
    lax.fori_loop(2, 3, second, 0)
    lax.fori_loop(0, 2, third, 0)
    swap(send_out, recv_out, out_send_sem, out_recv_sem, 0, 1, HALF)
    lax.fori_loop(3, CHUNKS + 1, second, 0)
    swap(send_out, recv_out, out_send_sem, out_recv_sem, 0, HALF, PEERS)
    lax.fori_loop(2, CHUNKS + 1, third, 0)

    def store(c):
        at = pl.ds(c * DEPTH, DEPTH)
        return pltpu.make_async_copy(outv.at[:, at], out_hbm.at[:, at], store_sem.at[c])

    def finish(c, _):
        pltpu.make_async_copy(recv_out.at[c], recv_out.at[c], out_recv_sem.at[c]).wait()
        for side in range(2):
            for gp in range(2):
                code = recv_out[c, side * 16 : side * 16 + 16, gp * 16 : gp * 16 + 16, :]
                level = code.astype(jnp.int32).astype(jnp.float32)
                for e in range(2):
                    block = level[:, e * 8 : e * 8 + 8, :].reshape(128, 128).T.astype(jnp.int32).astype(jnp.int16)
                    outv[2 * gp + e, pl.ds(c * DEPTH, DEPTH), side * ROWS : (side + 1) * ROWS, :] = block.reshape(
                        DEPTH, ROWS, 128
                    )
        store(c).start()
        return 0

    lax.fori_loop(0, CHUNKS, finish, 0)
    for c in range(CHUNKS):
        store(c).wait()
    most = pl.ds(0, PEERS - 1)
    pltpu.make_async_copy(send_in.at[:, most], send_in.at[:, most], in_send_sem).wait()
    pltpu.make_async_copy(send_out.at[:, most], send_out.at[:, most], out_send_sem).wait()
    pltpu.make_async_copy(rim_send, rim_send, rim_send_sem).wait()
    for n, count in ((0, 7), (1, 3)):
        sent = coef_recv.at[0, pl.ds(0, count)]
        pltpu.make_async_copy(sent, sent, coef_send_sem.at[n]).wait()


def per_device(n_gx, n_gy, noise, labels, pair_class, class_gain, stiffness, cross, current):
    hbm = pl.BlockSpec(memory_space=pl.ANY)
    dma = pltpu.SemaphoreType.DMA
    f32, bf16, i16 = jnp.float32, jnp.bfloat16, jnp.int16
    code = pl.pallas_call(
        functools.partial(exchange_kernel, n_gx, n_gy),
        out_shape=jax.ShapeDtypeStruct(noise.shape, i16),
        in_specs=[hbm] * 7,
        out_specs=hbm,
        scratch_shapes=[
            pltpu.VMEM((4, LAYERS, 64, 128), f32),
            pltpu.VMEM((LAYERS, ROWS, 128), jnp.int32),
            pltpu.VMEM((3, LAYERS, ROWS, 128), f32),
            pltpu.VMEM((128, 128), jnp.int32),
            pltpu.SMEM((4,), f32),
            pltpu.SMEM((3, 4), f32),
            pltpu.SMEM((4,), f32),
            pltpu.VMEM((4, LAYERS, 64, 128), i16),
            pltpu.VMEM((CHUNKS, PEERS, 32, 128), i16),
            pltpu.VMEM((CHUNKS, PEERS, 32, 128), i16),
            pltpu.VMEM((CHUNKS, PEERS, 32, 128), i16),
            pltpu.VMEM((CHUNKS, PEERS, 32, 128), i16),
            pltpu.VMEM((PEERS * 32, 128), f32),
            pltpu.VMEM((4, LAYERS * 10, 48, 128), f32),
            pltpu.VMEM((3, LAYERS * COLS, ROWS, 128), f32),
            pltpu.VMEM((DEPTH, COLS * ROWS, 128), f32),
            pltpu.VMEM((RIM_SLOTS, RIM_TOTAL, 128), bf16),
            pltpu.VMEM((RIM_SLOTS, RIM_TOTAL, 128), bf16),
            pltpu.VMEM((2, 8, 8, 128), f32),
            pltpu.VMEM((2, 8, 128), f32),
            pltpu.VMEM((5, 8, 128), f32),
            pltpu.VMEM((128, 128), bf16),
            dma((10,)),
            dma((CHUNKS,)),
            dma,
            dma((CHUNKS,)),
            dma,
            dma((CHUNKS,)),
            dma,
            dma((RIM_SLOTS,)),
            dma((2,)),
            dma((2,)),
        ],
        compiler_params=pltpu.CompilerParams(
            collective_id=0, has_side_effects=True, vmem_limit_bytes=60 * 1024 * 1024
        ),
        name="phase_steps",
    )(noise, labels, pair_class, class_gain, stiffness, cross, current)
    level = code.astype(f32) * (1.0 / CODE_K)
    size = jnp.exp2(jnp.abs(level)) * CODE_S - CODE_S
    return jnp.where(level < 0.0, -size, size)


def solution(mesh):
    placed = (
        P("ga", None, "gx", "gy"),
        P(None, "gx", "gy"),
        P(),
        P(),
        P(None, "ga"),
        P("ga"),
        P(None, None, "gx", "gy"),
    )
    return jax.shard_map(
        functools.partial(per_device, mesh.shape["gx"], mesh.shape["gy"]),
        mesh=mesh,
        in_specs=placed,
        out_specs=P("ga", None, "gx", "gy"),
        check_vma=False,
    )
```
